32 devices in a mesh: vol: 8 (over z, x), slab: 4 (over y, core).
Axes of the slice: x: 2, y: 2, z: 4, core: 2. Of those that a mesh axis runs over, the one named last changes fastest.
Arguments:
- face_disp: bfloat16 [64, 65536], P(None, ('vol', 'slab')), may hold values from -6 to 6
- contact_owner: int32 [65536, 1], P(('vol', 'slab')), may hold values from 0 to 7; in each aligned block of 2048 rows (0 to 2047, 2048 to 4095, ...) at most 1024 rows name the same one
- segment: int32 [65536], P(('vol', 'slab')), may hold values from 0 to 7
- face_area: float32 [65536], P(('vol', 'slab')), may hold values from 0.5 to 5
- face_nodes: int32 [4, 65536], P(None, ('vol', 'slab')), may hold values from 0 to 1023
- mortar_blocks: bfloat16 [256, 64, 64], P(('vol', 'slab')), may hold values from -0.75 to 0.75
- gap_offset: bfloat16 [256, 64], P(('vol', 'slab')), may hold values from -6 to 6
- shape_table: float32 [12, 64], replicated, may hold values from -0.75 to 0.75
- node_disp: float32 [3, 32768], P(None, ('vol', 'slab')), may hold values from -6 to 6
- stiffness: float32 [32768], P(('vol', 'slab')), may hold values from 0.2 to 2
- connect: int32 [8, 32768], P(None, ('vol', 'slab')), may hold values from 0 to 1023
- elem_matrix: float32 [24, 24], replicated, may hold values from -1.25 to 1.25
Outputs:
- residual: float32 [3, 32768], P(None, ('vol', 'slab'))
The draws below stay inside these ranges and needn't reach their ends.
Inputs may be any that keep to these rules, and one draw needn't show every extreme that they name: `contact_owner`: in each block of 2048 faces no owner index is named by more than 1024 faces, and some owner index is named by exactly 1024.
All inputs are finite; a program needn't handle non-finite values.
Results may differ from the reference program's by a relative error of at most 0.0028.
Values may be sent and summed in bfloat16 or wider, within the bound.
No kernel may reach another device: no remote copies, remote signals or barrier semaphores. Data moves between devices by JAX's collectives and lax.ppermute only.
A program may use at most 64 MiB of HBM per device.

```python
import math
import jax
import jax.numpy as jnp
import numpy as np
from jax import lax

K = 64
F_DEV = 2048
G = 8
NODE_DEV = 1024
SH = 256
CAP = 1024
FACES = 65536
SEGS = 256
NODES = 32768
ELEMS = 32768
N_VOL = 8
N_SLAB = 4


def set_ends(entries, rng, least, top_value):
    place = [jax.random.randint(jax.random.fold_in(rng, axis), (), 0, length) for axis, length in enumerate(entries.shape)]
    widest = entries.shape.index(max(entries.shape))
    neighbour = place[:widest] + [(place[widest] + 1) % entries.shape[widest]] + place[widest + 1:]
    return entries.at[tuple(place)].set(least).at[tuple(neighbour)].set(top_value)


def block_scale(key, dims, cuts, least, high):
    loudness, own = 1.0, jax.random.fold_in(key, 6)
    for dim, shards_of in cuts:
        heights = jnp.exp(jax.random.uniform(jax.random.fold_in(own, dim), (shards_of,), jnp.float32, least / len(cuts), high / len(cuts)))
        loudness = loudness * jnp.repeat(heights, dims[dim] // shards_of).reshape([-1 if axis == dim else 1 for axis in range(len(dims))])
    return loudness


def assign_block(stream_key, own, number, rows, number_of, top, limit, lean):
    sequence = jax.random.permutation(stream_key, number_of)
    crowded, ordinary = load_shares(number_of, rows * top, limit, lean, True), load_shares(number_of, rows * top, limit, lean, False)
    places = jnp.arange(number_of)

    def named(sizes, turn):
        used = int((sizes > 0).sum())
        fixed = max(1, used // 4)
        passed = fixed + (places - fixed + turn * (used - fixed)) % max(1, number_of - fixed)
        return jnp.zeros((number_of,), jnp.int32).at[sequence[jnp.where(places < fixed, places, passed)]].set(jnp.asarray(sizes, jnp.int32))

    sizes = jnp.where(number % 4 == 0, named(crowded, number // 4), named(ordinary, number - number // 4 - 1))
    mixed = jax.random.permutation(jax.random.fold_in(own, 3), number_of)
    source_of, receiver = mixed[0:number_of // 2 * 2:2], mixed[1:number_of // 2 * 2:2]
    room = jnp.minimum(sizes[source_of] - 1, limit - sizes[receiver]) // 2
    room = jnp.where((source_of == sequence[0]) | (receiver == sequence[0]) | (sizes[receiver] == 0), 0, jnp.maximum(room, 0))
    passed = jax.random.randint(jax.random.fold_in(own, 4), (number_of // 2,), 0, 1 << 20) % (room + 1)
    sizes = sizes.at[source_of].add(-passed).at[receiver].add(passed)
    members = jnp.searchsorted(jnp.cumsum(sizes), jnp.arange(rows * top), side="right").astype(jnp.int32)
    listing = members.reshape(top, rows).T
    listing = listing[jax.random.permutation(jax.random.fold_in(own, 1), rows)]
    turn = jax.random.randint(jax.random.fold_in(own, 2), (rows, 1), 0, top)
    return jnp.take_along_axis(listing, (jnp.arange(top)[None, :] + turn) % top, axis=1)


def load_shares(amount, total, reach, lean, full):
    portions = [(1 << 20) // math.isqrt(grade ** lean) + 1 for grade in range(1, amount + 1)]
    largest = reach if full else min(reach, max(-(-total // amount), total * portions[0] // sum(portions)))
    least = 1 if total - largest >= amount - 1 else 0
    given, surplus = [largest] + [least] * (amount - 1), total - largest - least * (amount - 1)
    while surplus > 0:
        candidates = [i for i in range(1, amount) if given[i] < largest] or [i for i in range(1, amount) if given[i] < reach]
        pool, remaining = sum([portions[i] for i in candidates]), surplus
        for i in candidates:
            more = min(reach - given[i], max(1, remaining * portions[i] // pool), surplus)
            given[i] = given[i] + more
            surplus = surplus - more
    return np.array(given)


def normal_values(own_key, shape, scale, most, cuts=(), held_as=jnp.bfloat16):
    values = jax.random.normal(own_key, shape, jnp.float32) * scale
    if len(cuts) > 0:
        values = block_scale(own_key, shape, cuts, -0.22, 0.18) * values
    return jnp.clip(values, min=-most, max=most).astype(held_as)


def setup_inputs(seed: int = 0) -> dict:
    streams_of = jax.random.split(jax.random.key(seed), 13)
    face_disp = normal_values(streams_of[0], (K, FACES), 1.0, 6.0, ((1, 32),))
    contact_owner_keys = jax.random.split(jax.random.fold_in(streams_of[1], 1), FACES // F_DEV)
    contact_owner_turns = jax.random.permutation(jax.random.fold_in(streams_of[1], 3), FACES // F_DEV)
    contact_owner = jax.vmap(lambda own, number: assign_block(jax.random.fold_in(streams_of[1], 2), own, number, F_DEV, N_VOL, 1, CAP, 2))(contact_owner_keys, contact_owner_turns).reshape((FACES, 1))
    segment = set_ends(jax.random.randint(streams_of[2], (FACES,), 0, G), jax.random.fold_in(streams_of[2], 1), 0, G - 1).astype(jnp.int32)
    face_area = jnp.clip(jnp.exp(math.log(5.0) - 2.3025851 * jax.random.uniform(streams_of[3], (FACES,), jnp.float32) ** block_scale(streams_of[3], (FACES,), ((0, 32),), -0.2, 0.2)), 0.5, 5.0)
    face_nodes = set_ends(jax.random.randint(streams_of[4], (4, FACES), 0, NODE_DEV), jax.random.fold_in(streams_of[4], 1), 0, NODE_DEV - 1).astype(jnp.int32)
    mortar_blocks = normal_values(streams_of[5], (SEGS, K, K), K ** -0.5, 0.75, ((0, 32),))
    gap_offset = normal_values(streams_of[6], (SEGS, K), 1.0, 6.0, ((0, 32),))
    shape_table = normal_values(streams_of[7], (12, K), K ** -0.5, 0.75, (), jnp.float32)
    node_disp = normal_values(streams_of[8], (3, NODES), 1.0, 6.0, ((1, 32),), jnp.float32)
    stiffness = jnp.clip(jnp.exp(math.log(2.0) - 2.3025851 * jax.random.uniform(streams_of[9], (ELEMS,), jnp.float32) ** block_scale(streams_of[9], (ELEMS,), ((0, 32),), -0.2, 0.2)), 0.2, 2.0)
    connect = set_ends(jax.random.randint(streams_of[10], (8, ELEMS), 0, NODE_DEV), jax.random.fold_in(streams_of[10], 1), 0, NODE_DEV - 1).astype(jnp.int32)
    elem_matrix = normal_values(streams_of[11], (24, 24), 24 ** -0.5, 1.25, (), jnp.float32)
    return dict(face_disp=face_disp, contact_owner=contact_owner, segment=segment, face_area=face_area, face_nodes=face_nodes, mortar_blocks=mortar_blocks, gap_offset=gap_offset, shape_table=shape_table, node_disp=node_disp, stiffness=stiffness, connect=connect, elem_matrix=elem_matrix)


highest = lax.Precision.HIGHEST


def reference(face_disp, contact_owner, segment, face_area, face_nodes, mortar_blocks, gap_offset, shape_table, node_disp, stiffness, connect, elem_matrix):
    device_count = N_VOL * N_SLAB
    face_block = jnp.arange(FACES, dtype=jnp.int32) // F_DEV
    slab_of = face_block % N_SLAB
    target = ((contact_owner[:, 0] * N_SLAB + slab_of) * G + segment).astype(jnp.int32)

    def by_device(array, row_count):
        return array.reshape(row_count, device_count, -1).transpose(1, 0, 2)

    def face_group(pieces):
        disp_block, target_block = pieces
        chosen = jnp.take(mortar_blocks, target_block, axis=0).astype(jnp.float32)
        offsets = jnp.take(gap_offset, target_block, axis=0).astype(jnp.float32).T
        gap = jnp.einsum("fij,jf->if", chosen, disp_block.astype(jnp.float32), precision=highest) - offsets
        traction = jax.nn.softplus(-gap)
        return jnp.einsum("fij,if->jf", chosen, traction, precision=highest).astype(jnp.bfloat16)

    seg_force = lax.map(face_group, (by_device(face_disp, K), target.reshape(device_count, F_DEV)))
    seg_force = seg_force.transpose(1, 0, 2).reshape(K, FACES)
    face_force = seg_force.astype(jnp.float32) * face_area[None, :]
    nodal_twelve = jnp.dot(shape_table, face_force, precision=highest, preferred_element_type=jnp.float32)

    def block_residual(pieces):
        node_block, conn_block, stiff_block, fnode_block, nodal_block = pieces
        elem_count = conn_block.shape[1]
        node_count = node_block.shape[1]
        face_count = fnode_block.shape[1]
        elem_disp = jnp.take(node_block, conn_block, axis=1).transpose(1, 0, 2).reshape(24, elem_count)
        elem_force = stiff_block[None, :] * jnp.dot(elem_matrix, elem_disp, precision=highest, preferred_element_type=jnp.float32)
        spread = elem_force.reshape(8, 3, elem_count).transpose(1, 0, 2).reshape(3, 8 * elem_count)
        internal = jnp.zeros((3, node_count), jnp.float32).at[:, conn_block.reshape(-1)].add(spread)
        pressed = nodal_block.reshape(4, 3, face_count).transpose(1, 0, 2).reshape(3, 4 * face_count)
        contact = jnp.zeros((3, node_count), jnp.float32).at[:, fnode_block.reshape(-1)].add(pressed)
        return internal - contact

    pieces = (by_device(node_disp, 3), by_device(connect, 8), stiffness.reshape(device_count, -1), by_device(face_nodes, 4), by_device(nodal_twelve, 12))
    unsummed = lax.map(block_residual, pieces)
    grid = unsummed.reshape(N_VOL, N_SLAB, 3, NODE_DEV)
    zero_rim = jnp.zeros((N_VOL, 1, 3, SH), jnp.float32)
    from_below = jnp.concatenate([zero_rim, grid[:, :-1, :, NODE_DEV - SH:]], axis=1)
    from_above = jnp.concatenate([grid[:, 1:, :, :SH], zero_rim], axis=1)
    lower = grid[:, :, :, :SH] + from_below
    upper = grid[:, :, :, NODE_DEV - SH:] + from_above
    summed = jnp.concatenate([lower, grid[:, :, :, SH:NODE_DEV - SH], upper], axis=3)
    return summed.transpose(2, 0, 1, 3).reshape(3, NODES)
```

```python
import jax
import jax.numpy as jnp
from jax import lax
from jax.experimental import pallas as pl
from jax.experimental.pallas import tpu as pltpu
from jax.sharding import PartitionSpec as P

SH = 256
LANES = 128
PACK_ROWS = 16
CHUNK = 16

f32, bf16, i32 = jnp.float32, jnp.bfloat16, jnp.int32


def split(values):
    high = values.astype(bf16)
    return high, (values - high.astype(f32)).astype(bf16)


def nt_dot(left, right):
    return lax.dot_general(left, right, (((1,), (1,)), ((), ())), preferred_element_type=f32)


def pack_kernel(mortar_ref, offset_ref, out_ref):
    segments, order, _ = mortar_ref.shape
    per_row = out_ref.shape[1] // order
    for first in range(0, segments, per_row):
        row = first // per_row * order
        blocks = [mortar_ref[first + place] for place in range(per_row)]
        out_ref[row : row + order, :] = jnp.concatenate(blocks, axis=1)
    rows = segments // per_row * order
    out_ref[rows:, :] = jnp.zeros((PACK_ROWS, out_ref.shape[1]), bf16)
    out_ref[rows : rows + segments, :order] = offset_ref[...]


def scatter_terms(value_rows, node_row, high_count):
    width = node_row.shape[1]
    high = jnp.broadcast_to(node_row // LANES, (high_count, width))
    mask = high == lax.broadcasted_iota(i32, (high_count, width), 0)
    rows = [jnp.where(mask, jnp.broadcast_to(v, (high_count, width)), 0.0) for v in value_rows]
    rows = jnp.concatenate(rows, axis=0)
    low = jnp.broadcast_to(node_row % LANES, (LANES, width))
    table = (low == lax.broadcasted_iota(i32, (LANES, width), 0)).astype(f32).astype(bf16)
    rows_high, rows_low = split(rows)
    return jnp.concatenate([rows_high, rows_low], axis=0), table


def element_kernel(disp_ref, connect_ref, stiffness_ref, matrix_ref, out_ref, elem_ref, force_ref):
    node_count = disp_ref.shape[1]
    elem_count = connect_ref.shape[1]
    corners = connect_ref.shape[0]
    high_count = node_count // LANES
    for start in range(0, elem_count, LANES):
        index = connect_ref[:, start : start + LANES]
        high, low = index // LANES, index % LANES
        for comp in range(3):
            picked = jnp.zeros(index.shape, f32)
            for part in range(high_count):
                line = disp_ref[comp : comp + 1, part * LANES : (part + 1) * LANES]
                table = jnp.broadcast_to(line, (corners, LANES))
                found = jnp.take_along_axis(table, low, axis=1, mode="promise_in_bounds")
                picked = jnp.where(high == part, found, picked)
            elem_ref[start // LANES, pl.ds(comp, corners, stride=3), :] = picked
    m_high, m_low = split(matrix_ref[...])
    d_high, d_low = split(jnp.concatenate([elem_ref[k] for k in range(elem_count // LANES)], axis=1))
    force = (
        jnp.dot(m_high, d_high, preferred_element_type=f32)
        + jnp.dot(m_high, d_low, preferred_element_type=f32)
        + jnp.dot(m_low, d_high, preferred_element_type=f32)
    )
    force_ref[...] = force * stiffness_ref[...]
    total = jnp.zeros((6 * high_count, LANES), f32)
    for corner in range(corners):
        values = [force_ref[3 * corner + c : 3 * corner + c + 1, :] for c in range(3)]
        rows, table = scatter_terms(values, connect_ref[corner : corner + 1, :], high_count)
        total = total + nt_dot(rows, table)
    out_ref[...] = total[: 3 * high_count] + total[3 * high_count :]


def contact_kernel(
    vol_ref, disp_ref, owner_ref, segment_ref, area_ref, nodes_ref, shape_ref, inner_ref, *rest, relative, tile
):
    payload_refs = rest[:-7]
    out_ref, edge_ref, far_ref, blocks_ref, offsets_ref, table_ref, nodal_ref = rest[-7:]
    order, faces = disp_ref.shape
    width = payload_refs[0].shape[1]
    per_row = width // order
    chunks = table_ref.shape[0]
    high_count = inner_ref.shape[0] // 3
    vol_count = offsets_ref.shape[1] // PACK_ROWS
    seg_rows = blocks_ref.shape[0] // vol_count
    groups = seg_rows // order
    piece = seg_rows + PACK_ROWS

    place = 0
    for ref in payload_refs:
        for start in range(0, ref.shape[0], piece):
            blocks_ref[place * seg_rows : (place + 1) * seg_rows, :] = ref[start : start + seg_rows, :]
            offsets_ref[:, place * PACK_ROWS : (place + 1) * PACK_ROWS] = jnp.transpose(
                ref[start + seg_rows : start + piece, :order].astype(f32)
            ).astype(bf16)
            place += 1

    sixteen = jnp.concatenate([shape_ref[...], jnp.zeros((16 - shape_ref.shape[0], order), f32)], axis=0)
    zero = jnp.zeros_like(sixteen)
    diagonal = jnp.concatenate(
        [jnp.concatenate([sixteen if r == c else zero for c in range(per_row)], axis=1) for r in range(per_row)],
        axis=0,
    )
    shape_high, shape_low = split(diagonal)
    shape_both = jnp.concatenate([shape_high, shape_low], axis=0)
    half = 16 * per_row
    quads = CHUNK // per_row

    def build(chunk, _):
        start = pl.multiple_of(chunk * (CHUNK * order), CHUNK * order)
        product = nt_dot(shape_both, blocks_ref[pl.ds(start, CHUNK * order), :])
        product = product[:half] + product[half:]
        for quad in range(quads):
            cut = product[:, quad * width : (quad + 1) * width]
            high, low = split(cut)
            both = jnp.concatenate([high, low], axis=0)
            table_ref[chunk, quad * 2 * half : (quad + 1) * 2 * half, :width] = both
            table_ref[chunk, quad * 2 * half : (quad + 1) * 2 * half, width:] = both
        return 0

    if chunks == 1:
        build(0, 0)
    else:
        lax.fori_loop(0, chunks, build, 0)

    def step(index, total):
        cols = pl.ds(pl.multiple_of(index * tile, tile), tile)
        owner = owner_ref[:, cols]
        segment = segment_ref[:, cols]
        if relative:
            owner = vol_ref[0] - owner
            owner = jnp.where(owner < 0, owner + vol_count, owner)
        slot = segment % per_row
        group = owner * groups + segment // per_row
        disp = disp_ref[:, cols]

        def masked(values, row, number):
            return values * (row == number).astype(f32).astype(bf16)

        spread = jnp.concatenate([masked(disp, slot, place) for place in range(per_row)], axis=0)
        target = owner * PACK_ROWS + segment
        picks = jnp.broadcast_to(target, (vol_count * PACK_ROWS, tile)) == lax.broadcasted_iota(
            i32, (vol_count * PACK_ROWS, tile), 0
        )
        gap = -jnp.dot(offsets_ref[...], picks.astype(f32).astype(bf16), preferred_element_type=f32)
        group_wide = jnp.broadcast_to(group, (order, tile))

        def add_gap(chunk, found):
            start = pl.multiple_of(chunk * (CHUNK * order), CHUNK * order)
            product = jnp.dot(blocks_ref[pl.ds(start, CHUNK * order), :], spread, preferred_element_type=f32)
            for place in range(CHUNK):
                found = jnp.where(
                    group_wide == chunk * CHUNK + place, product[place * order : (place + 1) * order], found
                )
            return found

        zero_gap = jnp.zeros((order, tile), f32)
        gap = gap + (add_gap(0, zero_gap) if chunks == 1 else lax.fori_loop(0, chunks, add_gap, zero_gap))
        pressure = -gap
        traction = jnp.maximum(pressure, 0.0) + jnp.log1p(jnp.exp(-jnp.abs(pressure)))
        t_high, t_low = split(traction)
        inner = group % per_row
        outer = (group // per_row) * per_row + slot
        pieces = [masked(t, inner, place) for t in (t_high, t_low) for place in range(per_row)]
        pressed = jnp.concatenate(pieces, axis=0)
        outer_wide = jnp.broadcast_to(outer, (16, tile))

        def add_nodal(chunk, found):
            product = jnp.dot(table_ref[chunk], pressed, preferred_element_type=f32)
            for quad in range(quads):
                for place in range(per_row):
                    row = quad * 2 * half + place * 16
                    value = product[row : row + 16] + product[row + half : row + half + 16]
                    number = (chunk * quads + quad) * per_row + place
                    found = jnp.where(outer_wide == number, value, found)
            return found

        zero_nodal = jnp.zeros((16, tile), f32)
        nodal = add_nodal(0, zero_nodal) if chunks == 1 else lax.fori_loop(0, chunks, add_nodal, zero_nodal)
        nodal_ref[...] = nodal * (-area_ref[:, cols])
        for corner in range(nodes_ref.shape[0]):
            values = [nodal_ref[3 * corner + c : 3 * corner + c + 1, :] for c in range(3)]
            rows, table = scatter_terms(values, nodes_ref[corner : corner + 1, cols], high_count)
            total = total + nt_dot(rows, table)
        return total

    total = lax.fori_loop(0, faces // tile, step, jnp.zeros((6 * high_count, LANES), f32))
    unsummed = total[: 3 * high_count] + total[3 * high_count :] + inner_ref[...]
    out_ref[...] = unsummed
    edge = edge_ref.shape[0] // 3
    lower = [unsummed[c * high_count : c * high_count + edge] for c in range(3)]
    upper = [unsummed[(c + 1) * high_count - edge : (c + 1) * high_count] for c in range(3)]
    lower, upper = jnp.concatenate(lower, axis=0), jnp.concatenate(upper, axis=0)
    odd = vol_ref[1] == 1
    edge_ref[...] = jnp.where(odd, lower, upper)
    far_ref[...] = jnp.where(odd, upper, lower)


def close_kernel(slab_ref, whole_ref, edge_ref, far_ref, out_ref):
    high_count = whole_ref.shape[0] // 3
    edge = edge_ref.shape[0] // 3
    odd = slab_ref[1] == 1
    lower = jnp.where(odd, edge_ref[...], far_ref[...])
    upper = jnp.where(odd, far_ref[...], edge_ref[...])
    whole = whole_ref[...]
    for c in range(3):
        for part in range(high_count):
            line = whole[c * high_count + part : c * high_count + part + 1]
            if part < edge:
                line = line + lower[c * edge + part : c * edge + part + 1]
            if part >= high_count - edge:
                near = c * edge + part - (high_count - edge)
                line = line + upper[near : near + 1]
            out_ref[c : c + 1, part * LANES : (part + 1) * LANES] = line


def vmem():
    return pl.BlockSpec(memory_space=pltpu.VMEM)


def smem():
    return pl.BlockSpec(memory_space=pltpu.SMEM)


def shards(
    face_disp,
    contact_owner,
    segment,
    face_area,
    face_nodes,
    mortar_blocks,
    gap_offset,
    shape_table,
    node_disp,
    stiffness,
    connect,
    elem_matrix,
):
    vol_count, slab_count = lax.axis_size("vol"), lax.axis_size("slab")
    segments, order, _ = mortar_blocks.shape
    faces = face_disp.shape[1]
    node_count = node_disp.shape[1]
    elem_count = connect.shape[1]
    high_count = node_count // LANES
    per_row = 256 // order
    seg_rows = segments // per_row * order
    width = per_row * order
    vol = lax.axis_index("vol")
    slab = lax.axis_index("slab")
    scalars = jnp.stack([vol, slab % 2]).astype(i32)

    payload = pl.pallas_call(
        pack_kernel,
        out_shape=jax.ShapeDtypeStruct((seg_rows + PACK_ROWS, width), bf16),
        in_specs=[vmem(), vmem()],
        out_specs=vmem(),
        name="pack",
    )(mortar_blocks, gap_offset)
    relative = vol_count <= 8
    if relative:
        payloads = [payload] + [
            lax.ppermute(payload, "vol", [(i, (i + k) % vol_count) for i in range(vol_count)])
            for k in range(1, vol_count)
        ]
    else:
        payloads = [lax.all_gather(payload, "vol", tiled=True)]

    internal = pl.pallas_call(
        element_kernel,
        out_shape=jax.ShapeDtypeStruct((3 * high_count, LANES), f32),
        in_specs=[vmem()] * 4,
        out_specs=vmem(),
        scratch_shapes=[pltpu.VMEM((elem_count // LANES, 24, LANES), f32), pltpu.VMEM((24, elem_count), f32)],
        cost_estimate=pl.CostEstimate(flops=2_000_000_000, bytes_accessed=100_000, transcendentals=0),
        name="element",
    )(node_disp, connect, stiffness[None, :], elem_matrix)

    chunks = vol_count * (segments // per_row) // CHUNK
    tile = min(512, faces)
    edge_rows = 3 * (SH // LANES)
    unsummed, edge, far = pl.pallas_call(
        lambda *refs: contact_kernel(*refs, relative=relative, tile=tile),
        out_shape=[
            jax.ShapeDtypeStruct((3 * high_count, LANES), f32),
            jax.ShapeDtypeStruct((edge_rows, LANES), f32),
            jax.ShapeDtypeStruct((edge_rows, LANES), f32),
        ],
        in_specs=[smem()] + [vmem()] * (7 + len(payloads)),
        out_specs=[vmem()] * 3,
        scratch_shapes=[
            pltpu.VMEM((vol_count * seg_rows, width), bf16),
            pltpu.VMEM((order, vol_count * PACK_ROWS), bf16),
            pltpu.VMEM((chunks, 2 * 16 * CHUNK, 2 * width), bf16),
            pltpu.VMEM((16, tile), f32),
        ],
        name="contact",
    )(
        scalars,
        face_disp,
        contact_owner.reshape(1, faces),
        segment[None, :],
        face_area[None, :],
        face_nodes,
        shape_table,
        internal,
        *payloads,
    )
    near_pairs = [(i, i + 1) for i in range(0, slab_count - 1, 2)]
    far_pairs = [(i, i + 1) for i in range(1, slab_count - 1, 2)]
    far_in = lax.ppermute(far, "slab", far_pairs + [(b, a) for a, b in far_pairs])
    edge_in = lax.ppermute(edge, "slab", near_pairs + [(b, a) for a, b in near_pairs])
    return pl.pallas_call(
        close_kernel,
        out_shape=jax.ShapeDtypeStruct((3, node_count), f32),
        in_specs=[smem()] + [vmem()] * 3,
        out_specs=vmem(),
        name="close",
    )(scalars, unsummed, edge_in, far_in)


def solution(mesh):
    in_specs = (
        P(None, ("vol", "slab")),
        P(("vol", "slab"), None),
        P(("vol", "slab")),
        P(("vol", "slab")),
        P(None, ("vol", "slab")),
        P(("vol", "slab"), None, None),
        P(("vol", "slab"), None),
        P(),
        P(None, ("vol", "slab")),
        P(("vol", "slab")),
        P(None, ("vol", "slab")),
        P(),
    )
    out_specs = P(None, ("vol", "slab"))
    return jax.shard_map(shards, mesh=mesh, in_specs=in_specs, out_specs=out_specs, check_vma=False)
```

```python
import functools

import jax
import jax.numpy as jnp
from jax import lax
from jax.experimental import pallas as pl
from jax.experimental.pallas import tpu as pltpu
from jax.sharding import PartitionSpec as P

SH = 256
LANES = 128
PACK_ROWS = 16
CHUNK = 16
LIMIT = 16 * 1024 * 1024

f32, bf16, i32 = jnp.float32, jnp.bfloat16, jnp.int32


def split(values):
    high = values.astype(bf16)
    return high, (values - high.astype(f32)).astype(bf16)


def nt_dot(left, right):
    return lax.dot_general(left, right, (((1,), (1,)), ((), ())), preferred_element_type=f32)


def low_table(node_row):
    shape = (LANES, node_row.shape[1])
    low = jnp.broadcast_to(node_row % LANES, shape)
    return (low == lax.broadcasted_iota(i32, shape, 0)).astype(f32).astype(bf16)


def scatter_rows(value_rows, high_row, high_count):
    shape = (high_count, high_row.shape[1])
    mask = jnp.broadcast_to(high_row, shape) == lax.broadcasted_iota(i32, shape, 0)
    rows = [jnp.where(mask, jnp.broadcast_to(v, shape), 0.0) for v in value_rows]
    return jnp.concatenate(split(jnp.concatenate(rows, axis=0)), axis=0)


def masked(values, row, number):
    return values * (row == number).astype(f32).astype(bf16)


def pack_kernel(mortar_ref, offset_ref, out_ref):
    segments, order, _ = mortar_ref.shape
    per_row = out_ref.shape[1] // order
    for first in range(0, segments, per_row):
        row = first // per_row * order
        blocks = [mortar_ref[first + place] for place in range(per_row)]
        out_ref[row : row + order, :] = jnp.concatenate(blocks, axis=1)
    rows = segments // per_row * order
    out_ref[rows:, :] = jnp.zeros((PACK_ROWS, out_ref.shape[1]), bf16)
    out_ref[rows : rows + segments, :order] = offset_ref[...]


def join_kernel(*refs):
    out_ref = refs[-1]
    place = 0
    for ref in refs[:-1]:
        if len(ref.shape) == 2 and ref.shape[1] == out_ref.shape[1]:
            out_ref[place : place + ref.shape[0], :] = ref[...]
            place += ref.shape[0]


def element_part(disp_ref, connect_ref, stiffness_ref, matrix_ref, out_ref, elem_ref, force_ref):
    node_count = disp_ref.shape[1]
    corners, elem_count = connect_ref.shape
    high_count = node_count // LANES
    for start in range(0, elem_count, LANES):
        index = connect_ref[:, start : start + LANES]
        high, low = index // LANES, index % LANES
        for comp in range(3):
            picked = jnp.zeros(index.shape, f32)
            for part in range(high_count):
                line = disp_ref[comp : comp + 1, part * LANES : (part + 1) * LANES]
                table = jnp.broadcast_to(line, (corners, LANES))
                found = jnp.take_along_axis(table, low, axis=1, mode="promise_in_bounds")
                picked = jnp.where(high == part, found, picked)
            elem_ref[start // LANES, pl.ds(comp, corners, stride=3), :] = picked
    m_high, m_low = split(matrix_ref[...])
    d_high, d_low = split(jnp.concatenate([elem_ref[k] for k in range(elem_count // LANES)], axis=1))
    force = (
        jnp.dot(m_high, d_high, preferred_element_type=f32)
        + jnp.dot(m_high, d_low, preferred_element_type=f32)
        + jnp.dot(m_low, d_high, preferred_element_type=f32)
    )
    force_ref[...] = force * stiffness_ref[...]
    total = jnp.zeros((6 * high_count, LANES), f32)
    for corner in range(corners):
        values = [force_ref[3 * corner + c : 3 * corner + c + 1, :] for c in range(3)]
        row = connect_ref[corner : corner + 1, :]
        total = total + nt_dot(scatter_rows(values, row // LANES, high_count), low_table(row))
    out_ref[...] = total[: 3 * high_count] + total[3 * high_count :]


def local_kernel(*refs, place_owner, groups):
    vol_ref, node_ref, connect_ref, stiff_ref, matrix_ref, shape_ref, owner_ref, segment_ref, face_area_ref, face_ref = refs[:10]
    table_ref, rows_ref, area_ref, nodes_ref, both_ref, inner_ref, elem_ref, force_ref = refs[10:]
    element_part(node_ref, connect_ref, stiff_ref, matrix_ref, inner_ref, elem_ref, force_ref)
    order = shape_ref.shape[1]
    per_row = both_ref.shape[1] // order
    segment = segment_ref[...]
    slot = segment % per_row
    rows_ref[0:1, :] = slot
    rows_ref[1:2, :] = segment
    for corner in range(face_ref.shape[0]):
        table_ref[corner * LANES : (corner + 1) * LANES, :] = low_table(face_ref[corner : corner + 1, :])
    for part, local in enumerate(place_owner(owner_ref[...], vol_ref[0])):
        group = jnp.where(local < 0, -1, local * groups + segment // per_row)
        first = 2 + 4 * part
        rows_ref[first : first + 1, :] = group
        rows_ref[first + 1 : first + 2, :] = jnp.where(local < 0, -1, group % per_row)
        rows_ref[first + 2 : first + 3, :] = jnp.where(local < 0, -1, (group // per_row) * per_row + slot)
        rows_ref[first + 3 : first + 4, :] = jnp.where(local < 0, -1, local * PACK_ROWS + segment)
    area_ref[...] = -face_area_ref[...]
    nodes_ref[...] = face_ref[...] // LANES
    sixteen = jnp.concatenate([shape_ref[...], jnp.zeros((16 - shape_ref.shape[0], order), f32)], axis=0)
    zero = jnp.zeros_like(sixteen)
    diagonal = [
        jnp.concatenate([sixteen if r == c else zero for c in range(per_row)], axis=1) for r in range(per_row)
    ]
    both_ref[...] = jnp.concatenate(split(jnp.concatenate(diagonal, axis=0)), axis=0)


def contact_kernel(*refs, payloads, past, last, part, owners, chunk, tile):
    refs = list(refs)

    def take(count):
        taken = refs[:count]
        del refs[:count]
        return taken

    payload_refs = take(payloads)
    disp_ref, rows_ref, both_ref = take(3)
    (past_ref,) = take(1) if past else (None,)
    if last:
        area_ref, nodes_ref, table_ref, inner_ref, parity_ref = take(5)
        out_ref, near_ref, far_ref = take(3)
    else:
        (out_ref,) = take(1)
    blocks_ref, offsets_ref, map_ref, nodal_ref = refs
    order, faces = disp_ref.shape
    width = blocks_ref.shape[1]
    block_rows = blocks_ref.shape[0] // owners
    piece = block_rows + PACK_ROWS
    per_row = width // order
    chunks = blocks_ref.shape[0] // order // chunk
    quads = chunk // per_row
    rows = chunk * order
    size = 16 * per_row

    def at(number, count):
        return pl.ds(number * count if isinstance(number, int) else pl.multiple_of(number * count, count), count)

    place = 0
    for ref in payload_refs:
        for begin in range(0, ref.shape[0], piece):
            blocks_ref[place * block_rows : (place + 1) * block_rows, :] = ref[begin : begin + block_rows, :]
            offsets_ref[:, place * PACK_ROWS : (place + 1) * PACK_ROWS] = jnp.transpose(
                ref[begin + block_rows : begin + piece, :order].astype(f32)
            ).astype(bf16)
            place += 1

    def build(number, _):
        product = nt_dot(both_ref[...], blocks_ref[at(number, rows), :])
        product = product[:size] + product[size:]
        for quad in range(quads):
            both = jnp.concatenate(split(product[:, quad * width : (quad + 1) * width]), axis=0)
            map_ref[number, quad * 2 * size : (quad + 1) * 2 * size, :] = both
        return 0

    if chunks == 1:
        build(0, 0)
    else:
        lax.fori_loop(0, chunks, build, 0)

    def step(index, total):
        cols = at(index, tile)
        slot = rows_ref[0:1, cols]
        group, inner, outer, target = [rows_ref[2 + 4 * part + k : 3 + 4 * part + k, cols] for k in range(4)]
        shape = (owners * PACK_ROWS, tile)
        picks = jnp.broadcast_to(target, shape) == lax.broadcasted_iota(i32, shape, 0)
        gap = -jnp.dot(offsets_ref[...], picks.astype(f32).astype(bf16), preferred_element_type=f32)
        group_wide = jnp.broadcast_to(group, (order, tile))
        spread = jnp.concatenate([masked(disp_ref[:, cols], slot, place) for place in range(per_row)], axis=0)

        def add_gap(number, found):
            product = jnp.dot(blocks_ref[at(number, rows), :], spread, preferred_element_type=f32)
            for place in range(chunk):
                value = product[place * order : (place + 1) * order]
                found = jnp.where(group_wide == number * chunk + place, value, found)
            return found

        zero_gap = jnp.zeros((order, tile), f32)
        gap = gap + (add_gap(0, zero_gap) if chunks == 1 else lax.fori_loop(0, chunks, add_gap, zero_gap))
        pressure = -gap
        traction = jnp.maximum(pressure, 0.0) + jnp.log(1.0 + jnp.exp(-jnp.abs(pressure)))
        traction = traction.astype(bf16)
        pressed = jnp.concatenate([masked(traction, inner, place) for place in range(per_row)], axis=0)
        outer_wide = jnp.broadcast_to(outer, (16, tile))

        def add_nodal(number, found):
            product = jnp.dot(map_ref[number], pressed, preferred_element_type=f32)
            for quad in range(quads):
                for place in range(per_row):
                    row = quad * 2 * size + place * 16
                    value = product[row : row + 16] + product[row + size : row + size + 16]
                    key = (number * quads + quad) * per_row + place
                    found = jnp.where(outer_wide == key, value, found)
            return found

        nodal = past_ref[:, cols] if past else jnp.zeros((16, tile), f32)
        nodal = add_nodal(0, nodal) if chunks == 1 else lax.fori_loop(0, chunks, add_nodal, nodal)
        if not last:
            out_ref[:, cols] = nodal
            return total
        high_count = inner_ref.shape[0] // 3
        nodal_ref[:, cols] = nodal * area_ref[:, cols]
        for corner in range(nodes_ref.shape[0]):
            values = [nodal_ref[3 * corner + c : 3 * corner + c + 1, cols] for c in range(3)]
            placed = scatter_rows(values, nodes_ref[corner : corner + 1, cols], high_count)
            total = total + nt_dot(placed, table_ref[corner * LANES : (corner + 1) * LANES, cols])
        return total

    total = jnp.zeros((2 * inner_ref.shape[0], LANES), f32) if last else 0
    if chunks == 1:
        for index in range(faces // tile):
            total = step(index, total)
    else:
        total = lax.fori_loop(0, faces // tile, step, total)
    if last:
        inner_rows = inner_ref.shape[0]
        unsummed = total[:inner_rows] + total[inner_rows:] + inner_ref[...]
        high_count = inner_rows // 3
        edge = near_ref.shape[1] // LANES
        odd = parity_ref[0] == 1
        for c in range(3):
            for high in range(high_count):
                line = unsummed[c * high_count + high : c * high_count + high + 1]
                out_ref[c : c + 1, high * LANES : (high + 1) * LANES] = line
            for high in range(edge):
                low = unsummed[c * high_count + high : c * high_count + high + 1]
                top = (c + 1) * high_count - edge + high
                up = unsummed[top : top + 1]
                lanes = slice(high * LANES, (high + 1) * LANES)
                near_ref[c : c + 1, lanes] = jnp.where(odd, low, up)
                far_ref[c : c + 1, lanes] = jnp.where(odd, up, low)


def vmem():
    return pl.BlockSpec(memory_space=pltpu.VMEM)


def smem():
    return pl.BlockSpec(memory_space=pltpu.SMEM)


def call(kernel, out_shape, specs, scratch=(), flops=0, limit=LIMIT):
    single = not isinstance(out_shape, (list, tuple))
    return pl.pallas_call(
        kernel,
        out_shape=out_shape,
        in_specs=specs,
        out_specs=vmem() if single else [vmem()] * len(out_shape),
        scratch_shapes=list(scratch),
        compiler_params=pltpu.CompilerParams(vmem_limit_bytes=limit),
        cost_estimate=pl.CostEstimate(flops=flops, bytes_accessed=1_000_000, transcendentals=0),
    )


def place_exchanged(owner, vol):
    apart = owner ^ vol
    late = (apart >= 4) & (apart % 2 == 1)
    early = jnp.where(apart < 4, apart, 2 + apart // 2)
    return [jnp.where(late, -1, early), jnp.where(late, (apart - 4) // 2, -1)]


def shards(
    face_disp,
    contact_owner,
    segment,
    face_area,
    face_nodes,
    mortar_blocks,
    gap_offset,
    shape_table,
    node_disp,
    stiffness,
    connect,
    elem_matrix,
):
    vol_count, slab_count = lax.axis_size("vol"), lax.axis_size("slab")
    segments, order, _ = mortar_blocks.shape
    faces = face_disp.shape[1]
    face_corners = face_nodes.shape[0]
    node_count = node_disp.shape[1]
    corners, elem_count = connect.shape
    high_count = node_count // LANES
    per_row = 256 // order
    groups = segments // per_row
    block_rows = groups * order
    width = per_row * order
    vol = lax.axis_index("vol").astype(i32).reshape(1)
    slab = lax.axis_index("slab")
    parity = (slab & 1).astype(i32).reshape(1)

    def payload_shape(owners):
        return jax.ShapeDtypeStruct((owners * (block_rows + PACK_ROWS), width), bf16)

    payload = call(pack_kernel, payload_shape(1), [vmem()] * 2, flops=20_000_000_000)(mortar_blocks, gap_offset)

    exchanged = vol_count == 8
    if exchanged:
        place_owner, counts = place_exchanged, [6, 2]
    else:
        place_owner, counts = (lambda owner, _: [owner]), [vol_count]

    sources = [
        node_disp,
        connect,
        stiffness[None, :],
        elem_matrix,
        shape_table,
        contact_owner.reshape(1, faces),
        segment[None, :],
        face_area[None, :],
        face_nodes,
    ]
    tables, rows, area, nodes, both, internal = call(
        functools.partial(local_kernel, place_owner=place_owner, groups=groups),
        [
            jax.ShapeDtypeStruct((face_corners * LANES, faces), bf16),
            jax.ShapeDtypeStruct((2 + 4 * len(counts), faces), i32),
            jax.ShapeDtypeStruct((1, faces), f32),
            jax.ShapeDtypeStruct((face_corners, faces), i32),
            jax.ShapeDtypeStruct((32 * per_row, width), bf16),
            jax.ShapeDtypeStruct((3 * high_count, LANES), f32),
        ],
        [smem()] + [vmem()] * len(sources),
        [pltpu.VMEM((elem_count // LANES, 3 * corners, LANES), f32), pltpu.VMEM((3 * corners, elem_count), f32)],
        flops=2_000_000_000,
    )(vol, *sources)

    if exchanged:
        def swap(values, mask):
            return lax.ppermute(values, "vol", [(i, i ^ mask) for i in range(vol_count)])

        def join(*pieces):
            owners = sum(piece.shape[0] for piece in pieces if piece.shape[1] == width) // (block_rows + PACK_ROWS)
            return call(join_kernel, payload_shape(owners), [vmem()] * len(pieces))(*pieces)

        beside = swap(payload, 1)
        far, middle = swap(payload, 6), swap(payload, 4)
        near = swap(join(payload, beside), 2)
        late = swap(join(middle, far, area), 1)
        parts = [[payload, beside, near, middle, far], [late]]
    else:
        parts = [[lax.all_gather(payload, "vol", tiled=True)]]

    tile = min(512, faces)
    nodal = None
    for part, pieces in enumerate(parts):
        past, last = part > 0, part == len(parts) - 1
        owners = counts[part]
        chunk = min(CHUNK, owners * groups)
        operands = pieces + [face_disp, rows, both]
        specs = [vmem()] * len(operands)
        outs = jax.ShapeDtypeStruct((16, faces), f32)
        if past:
            operands.append(nodal)
            specs.append(vmem())
        if last:
            operands += [area, nodes, tables, internal, parity]
            specs += [vmem()] * 4 + [smem()]
            outs = [
                jax.ShapeDtypeStruct((3, node_count), f32),
                jax.ShapeDtypeStruct((3, SH), f32),
                jax.ShapeDtypeStruct((3, SH), f32),
            ]
        nodal = call(
            functools.partial(
                contact_kernel,
                payloads=len(pieces),
                past=past,
                last=last,
                part=part,
                owners=owners,
                chunk=chunk,
                tile=tile,
            ),
            outs,
            specs,
            [
                pltpu.VMEM((owners * block_rows, width), bf16),
                pltpu.VMEM((order, owners * PACK_ROWS), bf16),
                pltpu.VMEM((owners * groups // chunk, 32 * chunk, width), bf16),
                pltpu.VMEM((16, faces), f32),
            ],
            flops=1_000_000_000,
        )(*operands)
    unsummed, near_out, far_out = nodal
    near_pairs = [(i, i + 1) for i in range(0, slab_count - 1, 2)]
    far_pairs = [(i, i + 1) for i in range(1, slab_count - 1, 2)]
    far_in = lax.ppermute(far_out, "slab", far_pairs + [(b, a) for a, b in far_pairs])
    near_in = lax.ppermute(near_out, "slab", near_pairs + [(b, a) for a, b in near_pairs])
    odd = parity[0] == 1
    lower = unsummed[:, :SH] + jnp.where(odd, near_in, far_in)
    upper = unsummed[:, node_count - SH :] + jnp.where(odd, far_in, near_in)
    return jnp.concatenate([lower, unsummed[:, SH : node_count - SH], upper], axis=1)


def solution(mesh):
    in_specs = (
        P(None, ("vol", "slab")),
        P(("vol", "slab"), None),
        P(("vol", "slab")),
        P(("vol", "slab")),
        P(None, ("vol", "slab")),
        P(("vol", "slab"), None, None),
        P(("vol", "slab"), None),
        P(),
        P(None, ("vol", "slab")),
        P(("vol", "slab")),
        P(None, ("vol", "slab")),
        P(),
    )
    out_specs = P(None, ("vol", "slab"))
    return jax.shard_map(shards, mesh=mesh, in_specs=in_specs, out_specs=out_specs, check_vma=False)
```

```python
import functools

import jax
import jax.numpy as jnp
from jax import lax
from jax.experimental import pallas as pl
from jax.experimental.pallas import tpu as pltpu
from jax.sharding import PartitionSpec as P

SH = 256
LANES = 128
PACK_ROWS = 8
CHUNK = 16
LIMIT = 16 * 1024 * 1024

f32, bf16, i32 = jnp.float32, jnp.bfloat16, jnp.int32


def split(values):
    high = values.astype(bf16)
    return high, (values - high.astype(f32)).astype(bf16)


def nt_dot(left, right):
    return lax.dot_general(left, right, (((1,), (1,)), ((), ())), preferred_element_type=f32)


def low_table(node_row):
    shape = (LANES, node_row.shape[1])
    low = jnp.broadcast_to(node_row % LANES, shape)
    return (low == lax.broadcasted_iota(i32, shape, 0)).astype(f32).astype(bf16)


def scatter_rows(value_rows, high_row, high_count):
    shape = (high_count, high_row.shape[1])
    mask = jnp.broadcast_to(high_row, shape) == lax.broadcasted_iota(i32, shape, 0)
    rows = [jnp.where(mask, jnp.broadcast_to(v, shape), 0.0) for v in value_rows]
    return jnp.concatenate(split(jnp.concatenate(rows, axis=0)), axis=0)


def masked(values, row, number):
    return values * (row == number).astype(f32).astype(bf16)


def lead_kernel(out_ref):
    out_ref[...] = jnp.zeros(out_ref.shape, f32)


def pack_kernel(mortar_ref, offset_ref, _, out_ref):
    segments, order, _ = mortar_ref.shape
    per_row = out_ref.shape[1] // order
    for first in range(0, segments, per_row):
        row = first // per_row * order
        blocks = [mortar_ref[first + place] for place in range(per_row)]
        out_ref[row : row + order, :] = jnp.concatenate(blocks, axis=1)
    rows = segments // per_row * order
    out_ref[rows:, :] = jnp.zeros((PACK_ROWS, out_ref.shape[1]), bf16)
    out_ref[rows : rows + segments, :order] = offset_ref[...]


def join_kernel(*refs):
    out_ref = refs[-1]
    place = 0
    for ref in refs[:-1]:
        if len(ref.shape) == 2 and ref.shape[1] == out_ref.shape[1]:
            out_ref[place : place + ref.shape[0], :] = ref[...]
            place += ref.shape[0]


def element_part(disp_ref, connect_ref, stiffness_ref, matrix_ref, out_ref, elem_ref, force_ref):
    node_count = disp_ref.shape[1]
    corners, elem_count = connect_ref.shape
    high_count = node_count // LANES
    for start in range(0, elem_count, LANES):
        index = connect_ref[:, start : start + LANES]
        high, low = index // LANES, index % LANES
        for comp in range(3):
            picked = jnp.zeros(index.shape, f32)
            for part in range(high_count):
                line = disp_ref[comp : comp + 1, part * LANES : (part + 1) * LANES]
                table = jnp.broadcast_to(line, (corners, LANES))
                found = jnp.take_along_axis(table, low, axis=1, mode="promise_in_bounds")
                picked = jnp.where(high == part, found, picked)
            elem_ref[start // LANES, pl.ds(comp, corners, stride=3), :] = picked
    m_high, m_low = split(matrix_ref[...])
    d_high, d_low = split(jnp.concatenate([elem_ref[k] for k in range(elem_count // LANES)], axis=1))
    force = (
        jnp.dot(m_high, d_high, preferred_element_type=f32)
        + jnp.dot(m_high, d_low, preferred_element_type=f32)
        + jnp.dot(m_low, d_high, preferred_element_type=f32)
    )
    force_ref[...] = force * stiffness_ref[...]
    total = jnp.zeros((6 * high_count, LANES), f32)
    for corner in range(corners):
        values = [force_ref[3 * corner + c : 3 * corner + c + 1, :] for c in range(3)]
        row = connect_ref[corner : corner + 1, :]
        total = total + nt_dot(scatter_rows(values, row // LANES, high_count), low_table(row))
    out_ref[...] = total[: 3 * high_count] + total[3 * high_count :]


def local_kernel(*refs, place_owner, groups):
    vol_ref, node_ref, connect_ref, stiff_ref, matrix_ref, shape_ref, owner_ref, segment_ref, face_area_ref, face_ref = refs[:10]
    table_ref, rows_ref, area_ref, nodes_ref, both_ref, inner_ref, elem_ref, force_ref = refs[10:]
    element_part(node_ref, connect_ref, stiff_ref, matrix_ref, inner_ref, elem_ref, force_ref)
    order = shape_ref.shape[1]
    per_row = both_ref.shape[1] // order
    segment = segment_ref[...]
    slot = segment % per_row
    rows_ref[0:1, :] = slot
    rows_ref[1:2, :] = segment
    for corner in range(face_ref.shape[0]):
        table_ref[corner * LANES : (corner + 1) * LANES, :] = low_table(face_ref[corner : corner + 1, :])
    for part, local in enumerate(place_owner(owner_ref[...], vol_ref[0])):
        group = jnp.where(local < 0, -1, local * groups + segment // per_row)
        first = 2 + 4 * part
        rows_ref[first : first + 1, :] = group
        rows_ref[first + 1 : first + 2, :] = jnp.where(local < 0, -1, group % per_row)
        rows_ref[first + 2 : first + 3, :] = jnp.where(local < 0, -1, (group // per_row) * per_row + slot)
        rows_ref[first + 3 : first + 4, :] = jnp.where(local < 0, -1, local * PACK_ROWS + segment)
    area_ref[...] = -face_area_ref[...]
    nodes_ref[...] = face_ref[...] // LANES
    sixteen = jnp.concatenate([shape_ref[...], jnp.zeros((16 - shape_ref.shape[0], order), f32)], axis=0)
    zero = jnp.zeros_like(sixteen)
    diagonal = [
        jnp.concatenate([sixteen if r == c else zero for c in range(per_row)], axis=1) for r in range(per_row)
    ]
    both_ref[...] = jnp.concatenate(split(jnp.concatenate(diagonal, axis=0)), axis=0)


def contact_kernel(*refs, payloads, past, last, part, owners, chunk, tile):
    refs = list(refs)

    def take(count):
        taken = refs[:count]
        del refs[:count]
        return taken

    payload_refs = take(payloads)
    disp_ref, rows_ref, both_ref = take(3)
    (past_ref,) = take(1) if past else (None,)
    if last:
        area_ref, nodes_ref, table_ref, inner_ref, parity_ref = take(5)
        out_ref, near_ref, far_ref = take(3)
    else:
        (out_ref,) = take(1)
    blocks_ref, offsets_ref, map_ref, nodal_ref = refs
    order, faces = disp_ref.shape
    width = blocks_ref.shape[1]
    block_rows = blocks_ref.shape[0] // owners
    piece = block_rows + PACK_ROWS
    per_row = width // order
    chunks = blocks_ref.shape[0] // order // chunk
    quads = chunk // per_row
    rows = chunk * order
    size = 16 * per_row

    def at(number, count):
        return pl.ds(number * count if isinstance(number, int) else pl.multiple_of(number * count, count), count)

    place = 0
    lines = []
    for ref in payload_refs:
        for begin in range(0, ref.shape[0], piece):
            blocks_ref[place * block_rows : (place + 1) * block_rows, :] = ref[begin : begin + block_rows, :]
            lines.append(ref[begin + block_rows : begin + piece, :order].astype(f32))
            place += 1
    offsets_ref[...] = jnp.transpose(jnp.concatenate(lines, axis=0)).astype(bf16)

    def build(number, _):
        product = nt_dot(both_ref[...], blocks_ref[at(number, rows), :])
        product = product[:size] + product[size:]
        for quad in range(quads):
            both = jnp.concatenate(split(product[:, quad * width : (quad + 1) * width]), axis=0)
            map_ref[number, quad * 2 * size : (quad + 1) * 2 * size, :] = both
        return 0

    if chunks == 1:
        build(0, 0)
    else:
        lax.fori_loop(0, chunks, build, 0)

    def step(index, total):
        cols = at(index, tile)
        slot = rows_ref[0:1, cols]
        group, inner, outer, target = [rows_ref[2 + 4 * part + k : 3 + 4 * part + k, cols] for k in range(4)]
        shape = (owners * PACK_ROWS, tile)
        picks = jnp.broadcast_to(target, shape) == lax.broadcasted_iota(i32, shape, 0)
        gap = -jnp.dot(offsets_ref[...], picks.astype(f32).astype(bf16), preferred_element_type=f32)
        group_wide = jnp.broadcast_to(group, (order, tile))
        spread = jnp.concatenate([masked(disp_ref[:, cols], slot, place) for place in range(per_row)], axis=0)

        def add_gap(number, found):
            product = jnp.dot(blocks_ref[at(number, rows), :], spread, preferred_element_type=f32)
            for place in range(chunk):
                value = product[place * order : (place + 1) * order]
                found = jnp.where(group_wide == number * chunk + place, value, found)
            return found

        zero_gap = jnp.zeros((order, tile), f32)
        gap = gap + (add_gap(0, zero_gap) if chunks == 1 else lax.fori_loop(0, chunks, add_gap, zero_gap))
        pressure = -gap
        traction = jnp.maximum(pressure, 0.0) + jnp.log(1.0 + jnp.exp(-jnp.abs(pressure)))
        traction = traction.astype(bf16)
        pressed = jnp.concatenate([masked(traction, inner, place) for place in range(per_row)], axis=0)
        outer_wide = jnp.broadcast_to(outer, (16, tile))

        def add_nodal(number, found):
            product = jnp.dot(map_ref[number], pressed, preferred_element_type=f32)
            for quad in range(quads):
                for place in range(per_row):
                    row = quad * 2 * size + place * 16
                    value = product[row : row + 16] + product[row + size : row + size + 16]
                    key = (number * quads + quad) * per_row + place
                    found = jnp.where(outer_wide == key, value, found)
            return found

        nodal = past_ref[:, cols] if past else jnp.zeros((16, tile), f32)
        nodal = add_nodal(0, nodal) if chunks == 1 else lax.fori_loop(0, chunks, add_nodal, nodal)
        if not last:
            out_ref[:, cols] = nodal
            return total
        high_count = inner_ref.shape[0] // 3
        nodal_ref[:, cols] = nodal * area_ref[:, cols]
        for corner in range(nodes_ref.shape[0]):
            values = [nodal_ref[3 * corner + c : 3 * corner + c + 1, cols] for c in range(3)]
            placed = scatter_rows(values, nodes_ref[corner : corner + 1, cols], high_count)
            total = total + nt_dot(placed, table_ref[corner * LANES : (corner + 1) * LANES, cols])
        return total

    total = jnp.zeros((2 * inner_ref.shape[0], LANES), f32) if last else 0
    if chunks == 1:
        for index in range(faces // tile):
            total = step(index, total)
    else:
        total = lax.fori_loop(0, faces // tile, step, total)
    if last:
        inner_rows = inner_ref.shape[0]
        unsummed = total[:inner_rows] + total[inner_rows:] + inner_ref[...]
        high_count = inner_rows // 3
        edge = near_ref.shape[1] // LANES
        odd = parity_ref[0] == 1
        for c in range(3):
            for high in range(high_count):
                line = unsummed[c * high_count + high : c * high_count + high + 1]
                out_ref[c : c + 1, high * LANES : (high + 1) * LANES] = line
            for high in range(edge):
                low = unsummed[c * high_count + high : c * high_count + high + 1]
                top = (c + 1) * high_count - edge + high
                up = unsummed[top : top + 1]
                lanes = slice(high * LANES, (high + 1) * LANES)
                near_ref[c : c + 1, lanes] = jnp.where(odd, low, up)
                far_ref[c : c + 1, lanes] = jnp.where(odd, up, low)


def vmem():
    return pl.BlockSpec(memory_space=pltpu.VMEM)


def smem():
    return pl.BlockSpec(memory_space=pltpu.SMEM)


def call(kernel, out_shape, specs, scratch=(), flops=0, limit=LIMIT):
    single = not isinstance(out_shape, (list, tuple))
    return pl.pallas_call(
        kernel,
        out_shape=out_shape,
        in_specs=specs,
        out_specs=vmem() if single else [vmem()] * len(out_shape),
        scratch_shapes=list(scratch),
        compiler_params=pltpu.CompilerParams(vmem_limit_bytes=limit),
        cost_estimate=pl.CostEstimate(flops=flops, bytes_accessed=1_000_000, transcendentals=0),
    )


def place_exchanged(owner, vol):
    apart = owner ^ vol
    late = (apart >= 4) & (apart % 2 == 1)
    early = jnp.where(apart < 4, (apart % 2) * 2 + apart // 2, 2 + apart // 2)
    return [jnp.where(late, -1, early), jnp.where(late, (apart - 4) // 2, -1)]


def shards(
    face_disp,
    contact_owner,
    segment,
    face_area,
    face_nodes,
    mortar_blocks,
    gap_offset,
    shape_table,
    node_disp,
    stiffness,
    connect,
    elem_matrix,
):
    vol_count, slab_count = lax.axis_size("vol"), lax.axis_size("slab")
    segments, order, _ = mortar_blocks.shape
    faces = face_disp.shape[1]
    face_corners = face_nodes.shape[0]
    node_count = node_disp.shape[1]
    corners, elem_count = connect.shape
    high_count = node_count // LANES
    per_row = 256 // order
    groups = segments // per_row
    block_rows = groups * order
    width = per_row * order
    vol = lax.axis_index("vol").astype(i32).reshape(1)
    slab = lax.axis_index("slab")
    parity = (slab & 1).astype(i32).reshape(1)

    def payload_shape(owners):
        return jax.ShapeDtypeStruct((owners * (block_rows + PACK_ROWS), width), bf16)

    lead = call(lead_kernel, jax.ShapeDtypeStruct((8, LANES), f32), [], flops=20_000_000_000)()
    payload = call(pack_kernel, payload_shape(1), [vmem()] * 3, flops=20_000_000_000)(mortar_blocks, gap_offset, lead)

    exchanged = vol_count == 8
    if exchanged:
        place_owner, counts = place_exchanged, [6, 2]
    else:
        place_owner, counts = (lambda owner, _: [owner]), [vol_count]

    sources = [
        node_disp,
        connect,
        stiffness[None, :],
        elem_matrix,
        shape_table,
        contact_owner.reshape(1, faces),
        segment[None, :],
        face_area[None, :],
        face_nodes,
    ]
    tables, rows, area, nodes, both, internal = call(
        functools.partial(local_kernel, place_owner=place_owner, groups=groups),
        [
            jax.ShapeDtypeStruct((face_corners * LANES, faces), bf16),
            jax.ShapeDtypeStruct((2 + 4 * len(counts), faces), i32),
            jax.ShapeDtypeStruct((1, faces), f32),
            jax.ShapeDtypeStruct((face_corners, faces), i32),
            jax.ShapeDtypeStruct((32 * per_row, width), bf16),
            jax.ShapeDtypeStruct((3 * high_count, LANES), f32),
        ],
        [smem()] + [vmem()] * len(sources),
        [pltpu.VMEM((elem_count // LANES, 3 * corners, LANES), f32), pltpu.VMEM((3 * corners, elem_count), f32)],
        flops=2_000_000_000,
    )(vol, *sources)

    if exchanged:
        def swap(values, mask):
            return lax.ppermute(values, "vol", [(i, i ^ mask) for i in range(vol_count)])

        def join(*pieces):
            owners = sum(piece.shape[0] for piece in pieces if piece.shape[1] == width) // (block_rows + PACK_ROWS)
            return call(join_kernel, payload_shape(owners), [vmem()] * len(pieces))(*pieces)

        far, middle, near = swap(payload, 6), swap(payload, 4), swap(payload, 2)
        early = swap(join(payload, near), 1)
        late = swap(join(middle, far, area), 1)
        parts = [[payload, near, early, middle, far], [late]]
    else:
        parts = [[lax.all_gather(payload, "vol", tiled=True)]]

    tile = min(512, faces)
    nodal = None
    for part, pieces in enumerate(parts):
        past, last = part > 0, part == len(parts) - 1
        owners = counts[part]
        chunk = min(CHUNK, owners * groups)
        operands = pieces + [face_disp, rows, both]
        specs = [vmem()] * len(operands)
        outs = jax.ShapeDtypeStruct((16, faces), f32)
        if past:
            operands.append(nodal)
            specs.append(vmem())
        if last:
            operands += [area, nodes, tables, internal, parity]
            specs += [vmem()] * 4 + [smem()]
            outs = [
                jax.ShapeDtypeStruct((3, node_count), f32),
                jax.ShapeDtypeStruct((3, SH), f32),
                jax.ShapeDtypeStruct((3, SH), f32),
            ]
        nodal = call(
            functools.partial(
                contact_kernel,
                payloads=len(pieces),
                past=past,
                last=last,
                part=part,
                owners=owners,
                chunk=chunk,
                tile=tile,
            ),
            outs,
            specs,
            [
                pltpu.VMEM((owners * block_rows, width), bf16),
                pltpu.VMEM((order, owners * PACK_ROWS), bf16),
                pltpu.VMEM((owners * groups // chunk, 32 * chunk, width), bf16),
                pltpu.VMEM((16, faces), f32),
            ],
            flops=1_000_000_000,
        )(*operands)
    unsummed, near_out, far_out = nodal
    near_pairs = [(i, i + 1) for i in range(0, slab_count - 1, 2)]
    far_pairs = [(i, i + 1) for i in range(1, slab_count - 1, 2)]
    if slab_count % 2 == 0:
        far_pairs.append((0, slab_count - 1))
    far_in = lax.ppermute(far_out, "slab", far_pairs + [(b, a) for a, b in far_pairs])
    near_in = lax.ppermute(near_out, "slab", near_pairs + [(b, a) for a, b in near_pairs])
    odd = parity[0] == 1
    inside = (slab > 0) & (slab < slab_count - 1) if slab_count % 2 == 0 else True
    far_in = jnp.where(inside, far_in, 0.0)
    lower = unsummed[:, :SH] + jnp.where(odd, near_in, far_in)
    upper = unsummed[:, node_count - SH :] + jnp.where(odd, far_in, near_in)
    return jnp.concatenate([lower, unsummed[:, SH : node_count - SH], upper], axis=1)


def solution(mesh):
    in_specs = (
        P(None, ("vol", "slab")),
        P(("vol", "slab"), None),
        P(("vol", "slab")),
        P(("vol", "slab")),
        P(None, ("vol", "slab")),
        P(("vol", "slab"), None, None),
        P(("vol", "slab"), None),
        P(),
        P(None, ("vol", "slab")),
        P(("vol", "slab")),
        P(None, ("vol", "slab")),
        P(),
    )
    out_specs = P(None, ("vol", "slab"))
    return jax.shard_map(shards, mesh=mesh, in_specs=in_specs, out_specs=out_specs, check_vma=False)
```

```python
import functools

import jax
import jax.numpy as jnp
from jax import lax
from jax.experimental import pallas as pl
from jax.experimental.pallas import tpu as pltpu
from jax.sharding import PartitionSpec as P

SH = 256
LANES = 128
PACK_ROWS = 8
CHUNK = 16
LIMIT = 16 * 1024 * 1024

f32, bf16, i32 = jnp.float32, jnp.bfloat16, jnp.int32


def split(values):
    high = values.astype(bf16)
    return high, (values - high.astype(f32)).astype(bf16)


def nt_dot(left, right):
    return lax.dot_general(left, right, (((1,), (1,)), ((), ())), preferred_element_type=f32)


def low_table(node_row):
    shape = (LANES, node_row.shape[1])
    low = jnp.broadcast_to(node_row % LANES, shape)
    return (low == lax.broadcasted_iota(i32, shape, 0)).astype(f32).astype(bf16)


def scatter_rows(highs, lows, high_row, high_count):
    shape = (high_count, high_row.shape[1])
    mask = jnp.broadcast_to(high_row, shape) == lax.broadcasted_iota(i32, shape, 0)
    rows = [jnp.where(mask, jnp.broadcast_to(v, shape), 0.0) for v in highs + lows]
    return jnp.concatenate(rows, axis=0).astype(bf16)


def store_split(ref, cols, values):
    high, low = split(values)
    size = values.shape[0]
    ref[:size, cols] = high.astype(f32)
    ref[size : 2 * size, cols] = low.astype(f32)


def split_rows(ref, corner, size, cols):
    rows = [3 * corner + c for c in range(3)]
    return [ref[r : r + 1, cols] for r in rows], [ref[size + r : size + r + 1, cols] for r in rows]


def masked(values, row, number):
    return values * (row == number).astype(f32).astype(bf16)


def lead_kernel(out_ref):
    out_ref[...] = jnp.zeros(out_ref.shape, f32)


def pack_kernel(mortar_ref, offset_ref, _, out_ref):
    segments, order, _ = mortar_ref.shape
    per_row = out_ref.shape[1] // order
    for first in range(0, segments, per_row):
        row = first // per_row * order
        blocks = [mortar_ref[first + place] for place in range(per_row)]
        out_ref[row : row + order, :] = jnp.concatenate(blocks, axis=1)
    rows = segments // per_row * order
    out_ref[rows:, :] = jnp.zeros((PACK_ROWS, out_ref.shape[1]), bf16)
    out_ref[rows : rows + segments, :order] = offset_ref[...]


def join_kernel(*refs):
    out_ref = refs[-1]
    place = 0
    for ref in refs[:-1]:
        if len(ref.shape) == 2 and ref.shape[1] == out_ref.shape[1]:
            out_ref[place : place + ref.shape[0], :] = ref[...]
            place += ref.shape[0]


def element_part(disp_ref, connect_ref, stiffness_ref, matrix_ref, out_ref, elem_ref, force_ref):
    node_count = disp_ref.shape[1]
    corners, elem_count = connect_ref.shape
    high_count = node_count // LANES
    for start in range(0, elem_count, LANES):
        index = connect_ref[:, start : start + LANES]
        high, low = index // LANES, index % LANES
        for comp in range(3):
            picked = jnp.zeros(index.shape, f32)
            for part in range(high_count):
                line = disp_ref[comp : comp + 1, part * LANES : (part + 1) * LANES]
                table = jnp.broadcast_to(line, (corners, LANES))
                found = jnp.take_along_axis(table, low, axis=1, mode="promise_in_bounds")
                picked = jnp.where(high == part, found, picked)
            elem_ref[start // LANES, pl.ds(comp, corners, stride=3), :] = picked
    m_high, m_low = split(matrix_ref[...])
    d_high, d_low = split(jnp.concatenate([elem_ref[k] for k in range(elem_count // LANES)], axis=1))
    force = (
        jnp.dot(m_high, d_high, preferred_element_type=f32)
        + jnp.dot(m_high, d_low, preferred_element_type=f32)
        + jnp.dot(m_low, d_high, preferred_element_type=f32)
    )
    every = slice(0, elem_count)
    store_split(force_ref, every, force * stiffness_ref[...])
    total = jnp.zeros((6 * high_count, LANES), f32)
    for corner in range(corners):
        row = connect_ref[corner : corner + 1, :]
        placed = scatter_rows(*split_rows(force_ref, corner, 3 * corners, every), row // LANES, high_count)
        total = total + nt_dot(placed, low_table(row))
    out_ref[...] = total[: 3 * high_count] + total[3 * high_count :]


def local_kernel(*refs, place_owner, groups):
    vol_ref, odd_ref, node_ref, connect_ref, stiff_ref, matrix_ref, shape_ref, owner_ref, segment_ref, face_area_ref, face_ref = refs[:11]
    table_ref, rows_ref, area_ref, nodes_ref, both_ref, inner_ref, elem_ref, force_ref = refs[11:]
    element_part(node_ref, connect_ref, stiff_ref, matrix_ref, inner_ref, elem_ref, force_ref)
    order = shape_ref.shape[1]
    per_row = both_ref.shape[1] // order
    segment = segment_ref[...]
    slot = segment % per_row
    rows_ref[0:1, :] = slot
    rows_ref[1:2, :] = segment
    for corner in range(face_ref.shape[0]):
        table_ref[corner * LANES : (corner + 1) * LANES, :] = low_table(face_ref[corner : corner + 1, :])
    for part, local in enumerate(place_owner(owner_ref[...], vol_ref[0], odd_ref[0])):
        group = jnp.where(local < 0, -1, local * groups + segment // per_row)
        first = 2 + 4 * part
        rows_ref[first : first + 1, :] = group
        rows_ref[first + 1 : first + 2, :] = jnp.where(local < 0, -1, group % per_row)
        rows_ref[first + 2 : first + 3, :] = jnp.where(local < 0, -1, (group // per_row) * per_row + slot)
        rows_ref[first + 3 : first + 4, :] = jnp.where(local < 0, -1, local * PACK_ROWS + segment)
    area_ref[...] = -face_area_ref[...]
    nodes_ref[...] = face_ref[...] // LANES
    sixteen = jnp.concatenate([shape_ref[...], jnp.zeros((16 - shape_ref.shape[0], order), f32)], axis=0)
    zero = jnp.zeros_like(sixteen)
    diagonal = [
        jnp.concatenate([sixteen if r == c else zero for c in range(per_row)], axis=1) for r in range(per_row)
    ]
    both_ref[...] = jnp.concatenate(split(jnp.concatenate(diagonal, axis=0)), axis=0)


def contact_kernel(*refs, payloads, past, last, part, owners, chunk, tile):
    refs = list(refs)

    def take(count):
        taken = refs[:count]
        del refs[:count]
        return taken

    payload_refs = take(payloads)
    disp_ref, rows_ref, both_ref = take(3)
    (past_ref,) = take(1) if past else (None,)
    if last:
        area_ref, nodes_ref, table_ref, inner_ref, parity_ref = take(5)
        out_ref, near_ref, far_ref = take(3)
    else:
        (out_ref,) = take(1)
    blocks_ref, offsets_ref, map_ref, nodal_ref = refs
    order, faces = disp_ref.shape
    width = blocks_ref.shape[1]
    block_rows = blocks_ref.shape[0] // owners
    piece = block_rows + PACK_ROWS
    per_row = width // order
    chunks = blocks_ref.shape[0] // order // chunk
    quads = chunk // per_row
    rows = chunk * order
    size = 16 * per_row

    def at(number, count):
        return pl.ds(number * count if isinstance(number, int) else pl.multiple_of(number * count, count), count)

    place = 0
    lines = []
    for ref in payload_refs:
        for begin in range(0, ref.shape[0], piece):
            blocks_ref[place * block_rows : (place + 1) * block_rows, :] = ref[begin : begin + block_rows, :]
            lines.append(ref[begin + block_rows : begin + piece, :order].astype(f32))
            place += 1
    offsets_ref[...] = jnp.transpose(jnp.concatenate(lines, axis=0)).astype(bf16)

    def build(number, _):
        product = nt_dot(both_ref[...], blocks_ref[at(number, rows), :])
        product = product[:size] + product[size:]
        for quad in range(quads):
            both = jnp.concatenate(split(product[:, quad * width : (quad + 1) * width]), axis=0)
            map_ref[number, quad * 2 * size : (quad + 1) * 2 * size, :] = both
        return 0

    if chunks == 1:
        build(0, 0)
    else:
        lax.fori_loop(0, chunks, build, 0)

    def find_gap(index):
        cols = at(index, tile)
        slot = rows_ref[0:1, cols]
        group, inner, outer, target = [rows_ref[2 + 4 * part + k : 3 + 4 * part + k, cols] for k in range(4)]
        shape = (owners * PACK_ROWS, tile)
        picks = jnp.broadcast_to(target, shape) == lax.broadcasted_iota(i32, shape, 0)
        gap = -jnp.dot(offsets_ref[...], picks.astype(f32).astype(bf16), preferred_element_type=f32)
        group_wide = jnp.broadcast_to(group, (order, tile))
        spread = jnp.concatenate([masked(disp_ref[:, cols], slot, place) for place in range(per_row)], axis=0)

        def add_gap(number, found):
            product = jnp.dot(blocks_ref[at(number, rows), :], spread, preferred_element_type=f32)
            for place in range(chunk):
                value = product[place * order : (place + 1) * order]
                found = jnp.where(group_wide == number * chunk + place, value, found)
            return found

        zero_gap = jnp.zeros((order, tile), f32)
        gap = gap + (add_gap(0, zero_gap) if chunks == 1 else lax.fori_loop(0, chunks, add_gap, zero_gap))
        return index, gap, inner, outer

    def find_nodal(index, gap, inner, outer):
        cols = at(index, tile)
        pressure = -gap
        traction = jnp.maximum(pressure, 0.0) + jnp.log(1.0 + jnp.exp(-jnp.abs(pressure)))
        traction = traction.astype(bf16)
        pressed = jnp.concatenate([masked(traction, inner, place) for place in range(per_row)], axis=0)
        outer_wide = jnp.broadcast_to(outer, (16, tile))

        def add_nodal(number, found):
            product = jnp.dot(map_ref[number], pressed, preferred_element_type=f32)
            for quad in range(quads):
                for place in range(per_row):
                    row = quad * 2 * size + place * 16
                    value = product[row : row + 16] + product[row + size : row + size + 16]
                    key = (number * quads + quad) * per_row + place
                    found = jnp.where(outer_wide == key, value, found)
            return found

        nodal = past_ref[:, cols] if past else jnp.zeros((16, tile), f32)
        nodal = add_nodal(0, nodal) if chunks == 1 else lax.fori_loop(0, chunks, add_nodal, nodal)
        if not last:
            out_ref[:, cols] = nodal
        else:
            store_split(nodal_ref, cols, nodal * area_ref[:, cols])

    def scatter(index, total):
        if not last:
            return total
        cols = at(index, tile)
        high_count = inner_ref.shape[0] // 3
        placed, tables = [], []
        for corner in range(nodes_ref.shape[0]):
            halves = split_rows(nodal_ref, corner, 16, cols)
            placed.append(scatter_rows(*halves, nodes_ref[corner : corner + 1, cols], high_count))
            tables.append(table_ref[corner * LANES : (corner + 1) * LANES, cols])
        return total + nt_dot(jnp.concatenate(placed, axis=1), jnp.concatenate(tables, axis=1))

    total = jnp.zeros((2 * inner_ref.shape[0], LANES), f32) if last else 0
    count = faces // tile
    if chunks == 1:
        found = {}
        for turn in range(count + 2):
            if turn < count:
                found[turn] = find_gap(turn)
            if 0 <= turn - 1 < count:
                find_nodal(*found.pop(turn - 1))
            if 0 <= turn - 2:
                total = scatter(turn - 2, total)
    else:

        def step(index, total):
            find_nodal(*find_gap(index))
            return scatter(index, total)

        total = lax.fori_loop(0, count, step, total)
    if last:
        inner_rows = inner_ref.shape[0]
        unsummed = total[:inner_rows] + total[inner_rows:] + inner_ref[...]
        high_count = inner_rows // 3
        edge = near_ref.shape[1] // LANES
        odd = parity_ref[0] == 1
        for c in range(3):
            for high in range(high_count):
                line = unsummed[c * high_count + high : c * high_count + high + 1]
                out_ref[c : c + 1, high * LANES : (high + 1) * LANES] = line
            for high in range(edge):
                low = unsummed[c * high_count + high : c * high_count + high + 1]
                top = (c + 1) * high_count - edge + high
                up = unsummed[top : top + 1]
                lanes = slice(high * LANES, (high + 1) * LANES)
                near_ref[c : c + 1, lanes] = jnp.where(odd, low, up)
                far_ref[c : c + 1, lanes] = jnp.where(odd, up, low)


def vmem():
    return pl.BlockSpec(memory_space=pltpu.VMEM)


def smem():
    return pl.BlockSpec(memory_space=pltpu.SMEM)


def call(kernel, out_shape, specs, scratch=(), flops=0, limit=LIMIT):
    single = not isinstance(out_shape, (list, tuple))
    return pl.pallas_call(
        kernel,
        out_shape=out_shape,
        in_specs=specs,
        out_specs=vmem() if single else [vmem()] * len(out_shape),
        scratch_shapes=list(scratch),
        compiler_params=pltpu.CompilerParams(vmem_limit_bytes=limit),
        cost_estimate=pl.CostEstimate(flops=flops, bytes_accessed=1_000_000, transcendentals=0),
    )


ORDERS = ((2, 4, 6), (4, 6, 2))


def place_exchanged(owner, vol, odd_slab):
    apart = owner ^ vol
    beside, pair = apart % 2, apart // 2
    turned = jnp.where(pair == 0, 0, (pair + 1) % 3 + 1)
    step = jnp.where(odd_slab == 1, turned, pair)
    late = (step >= 2) & (beside == 1)
    early = jnp.where(step < 2, beside * 2 + step, step + 2)
    return [jnp.where(late, -1, early), jnp.where(late, step - 2, -1)]


def shards(
    face_disp,
    contact_owner,
    segment,
    face_area,
    face_nodes,
    mortar_blocks,
    gap_offset,
    shape_table,
    node_disp,
    stiffness,
    connect,
    elem_matrix,
):
    vol_count, slab_count = lax.axis_size("vol"), lax.axis_size("slab")
    segments, order, _ = mortar_blocks.shape
    faces = face_disp.shape[1]
    face_corners = face_nodes.shape[0]
    node_count = node_disp.shape[1]
    corners, elem_count = connect.shape
    high_count = node_count // LANES
    per_row = 256 // order
    groups = segments // per_row
    block_rows = groups * order
    width = per_row * order
    vol = lax.axis_index("vol").astype(i32).reshape(1)
    slab = lax.axis_index("slab")
    parity = (slab & 1).astype(i32).reshape(1)

    def payload_shape(owners):
        return jax.ShapeDtypeStruct((owners * (block_rows + PACK_ROWS), width), bf16)

    lead = call(lead_kernel, jax.ShapeDtypeStruct((8, LANES), f32), [], flops=20_000_000_000)()
    payload = call(pack_kernel, payload_shape(1), [vmem()] * 3, flops=20_000_000_000)(mortar_blocks, gap_offset, lead)

    exchanged = vol_count == 8
    if exchanged:
        place_owner, counts = place_exchanged, [6, 2]
    else:
        place_owner, counts = (lambda owner, *_: [owner]), [vol_count]

    sources = [
        node_disp,
        connect,
        stiffness[None, :],
        elem_matrix,
        shape_table,
        contact_owner.reshape(1, faces),
        segment[None, :],
        face_area[None, :],
        face_nodes,
    ]
    tables, rows, area, nodes, both, internal = call(
        functools.partial(local_kernel, place_owner=place_owner, groups=groups),
        [
            jax.ShapeDtypeStruct((face_corners * LANES, faces), bf16),
            jax.ShapeDtypeStruct((2 + 4 * len(counts), faces), i32),
            jax.ShapeDtypeStruct((1, faces), f32),
            jax.ShapeDtypeStruct((face_corners, faces), i32),
            jax.ShapeDtypeStruct((32 * per_row, width), bf16),
            jax.ShapeDtypeStruct((3 * high_count, LANES), f32),
        ],
        [smem()] * 2 + [vmem()] * len(sources),
        [pltpu.VMEM((elem_count // LANES, 3 * corners, LANES), f32), pltpu.VMEM((6 * corners, elem_count), f32)],
        flops=2_000_000_000,
    )(vol, parity, *sources)

    if exchanged:
        def swap(values, masks):
            pairs = [
                (v * slab_count + s, (v ^ masks[s % 2]) * slab_count + s)
                for v in range(vol_count)
                for s in range(slab_count)
            ]
            return lax.ppermute(values, ("vol", "slab"), pairs)

        def join(*pieces):
            owners = sum(piece.shape[0] for piece in pieces if piece.shape[1] == width) // (block_rows + PACK_ROWS)
            return call(join_kernel, payload_shape(owners), [vmem()] * len(pieces))(*pieces)

        one, two, three = [swap(payload, masks) for masks in zip(*ORDERS)]
        early = swap(join(payload, one), (1, 1))
        late = [swap(join(two, area), (1, 1)), swap(three, (1, 1))]
        parts = [[payload, one, early, two, three], late]
    else:
        parts = [[lax.all_gather(payload, "vol", tiled=True)]]

    nodal = None
    for part, pieces in enumerate(parts):
        past, last = part > 0, part == len(parts) - 1
        owners = counts[part]
        chunk = min(CHUNK, owners * groups)
        tile = min(256 if last else 512, faces)
        operands = pieces + [face_disp, rows, both]
        specs = [vmem()] * len(operands)
        outs = jax.ShapeDtypeStruct((16, faces), f32)
        if past:
            operands.append(nodal)
            specs.append(vmem())
        if last:
            operands += [area, nodes, tables, internal, parity]
            specs += [vmem()] * 4 + [smem()]
            outs = [
                jax.ShapeDtypeStruct((3, node_count), f32),
                jax.ShapeDtypeStruct((3, SH), f32),
                jax.ShapeDtypeStruct((3, SH), f32),
            ]
        nodal = call(
            functools.partial(
                contact_kernel,
                payloads=len(pieces),
                past=past,
                last=last,
                part=part,
                owners=owners,
                chunk=chunk,
                tile=tile,
            ),
            outs,
            specs,
            [
                pltpu.VMEM((owners * block_rows, width), bf16),
                pltpu.VMEM((order, owners * PACK_ROWS), bf16),
                pltpu.VMEM((owners * groups // chunk, 32 * chunk, width), bf16),
                pltpu.VMEM((32, faces), f32),
            ],
            flops=1_000_000_000,
        )(*operands)
    unsummed, near_out, far_out = nodal
    near_pairs = [(i, i + 1) for i in range(0, slab_count - 1, 2)]
    far_pairs = [(i, i + 1) for i in range(1, slab_count - 1, 2)]
    if slab_count % 2 == 0:
        far_pairs.append((0, slab_count - 1))
    far_in = lax.ppermute(far_out, "slab", far_pairs + [(b, a) for a, b in far_pairs])
    near_in = lax.ppermute(near_out, "slab", near_pairs + [(b, a) for a, b in near_pairs])
    odd = parity[0] == 1
    inside = (slab > 0) & (slab < slab_count - 1) if slab_count % 2 == 0 else True
    far_in = jnp.where(inside, far_in, 0.0)
    lower = unsummed[:, :SH] + jnp.where(odd, near_in, far_in)
    upper = unsummed[:, node_count - SH :] + jnp.where(odd, far_in, near_in)
    return jnp.concatenate([lower, unsummed[:, SH : node_count - SH], upper], axis=1)


def solution(mesh):
    in_specs = (
        P(None, ("vol", "slab")),
        P(("vol", "slab"), None),
        P(("vol", "slab")),
        P(("vol", "slab")),
        P(None, ("vol", "slab")),
        P(("vol", "slab"), None, None),
        P(("vol", "slab"), None),
        P(),
        P(None, ("vol", "slab")),
        P(("vol", "slab")),
        P(None, ("vol", "slab")),
        P(),
    )
    out_specs = P(None, ("vol", "slab"))
    return jax.shard_map(shards, mesh=mesh, in_specs=in_specs, out_specs=out_specs, check_vma=False)
```

```python
import functools

import jax
import jax.numpy as jnp
from jax import lax
from jax.experimental import pallas as pl
from jax.experimental.pallas import tpu as pltpu
from jax.sharding import PartitionSpec as P

SH = 256
LANES = 128
PACK_ROWS = 8
CHUNK = 16
LIMIT = 16 * 1024 * 1024

f32, bf16, i32 = jnp.float32, jnp.bfloat16, jnp.int32


def split(values):
    high = values.astype(bf16)
    return high, (values - high.astype(f32)).astype(bf16)


def nt_dot(left, right):
    return lax.dot_general(left, right, (((1,), (1,)), ((), ())), preferred_element_type=f32)


def low_table(node_row):
    shape = (LANES, node_row.shape[1])
    low = jnp.broadcast_to((node_row % LANES).astype(f32).astype(bf16), shape)
    lines = lax.broadcasted_iota(i32, shape, 0).astype(f32).astype(bf16)
    return jnp.where(low == lines, jnp.ones((), bf16), jnp.zeros((), bf16))


def scatter_rows(highs, lows, high_row, high_count):
    shape = (high_count, high_row.shape[1])
    mask = jnp.broadcast_to(high_row, shape) == lax.broadcasted_iota(i32, shape, 0)
    rows = [jnp.where(mask, jnp.broadcast_to(v, shape), 0.0) for v in highs + lows]
    return jnp.concatenate(rows, axis=0).astype(bf16)


def store_split(ref, cols, values):
    high, low = split(values)
    size = values.shape[0]
    ref[:size, cols] = high.astype(f32)
    ref[size : 2 * size, cols] = low.astype(f32)


def split_rows(ref, corner, size, cols):
    rows = [3 * corner + c for c in range(3)]
    return [ref[r : r + 1, cols] for r in rows], [ref[size + r : size + r + 1, cols] for r in rows]


def masked(values, row, number):
    return values * (row == number).astype(f32).astype(bf16)


def lead_kernel(out_ref):
    out_ref[...] = jnp.zeros(out_ref.shape, f32)


def pack_kernel(mortar_ref, offset_ref, _, out_ref):
    segments, order, _ = mortar_ref.shape
    per_row = out_ref.shape[1] // order
    for first in range(0, segments, per_row):
        row = first // per_row * order
        blocks = [mortar_ref[first + place] for place in range(per_row)]
        out_ref[row : row + order, :] = jnp.concatenate(blocks, axis=1)
    rows = segments // per_row * order
    out_ref[rows:, :] = jnp.zeros((PACK_ROWS, out_ref.shape[1]), bf16)
    out_ref[rows : rows + segments, :order] = offset_ref[...]


def join_kernel(*refs):
    out_ref = refs[-1]
    place = 0
    for ref in refs[:-1]:
        if len(ref.shape) == 2 and ref.shape[1] == out_ref.shape[1]:
            out_ref[place : place + ref.shape[0], :] = ref[...]
            place += ref.shape[0]


def element_kernel(disp_ref, connect_ref, stiffness_ref, matrix_ref, out_ref, elem_ref, force_ref):
    node_count = disp_ref.shape[1]
    corners, elem_count = connect_ref.shape
    high_count = node_count // LANES
    for start in range(0, elem_count, LANES):
        index = connect_ref[:, start : start + LANES]
        high, low = index // LANES, index % LANES
        for comp in range(3):
            picked = jnp.zeros(index.shape, f32)
            for part in range(high_count):
                line = disp_ref[comp : comp + 1, part * LANES : (part + 1) * LANES]
                table = jnp.broadcast_to(line, (corners, LANES))
                found = jnp.take_along_axis(table, low, axis=1, mode="promise_in_bounds")
                picked = jnp.where(high == part, found, picked)
            elem_ref[start // LANES, pl.ds(comp, corners, stride=3), :] = picked
    m_high, m_low = split(matrix_ref[...])
    d_high, d_low = split(jnp.concatenate([elem_ref[k] for k in range(elem_count // LANES)], axis=1))
    force = (
        jnp.dot(m_high, d_high, preferred_element_type=f32)
        + jnp.dot(m_high, d_low, preferred_element_type=f32)
        + jnp.dot(m_low, d_high, preferred_element_type=f32)
    )
    every = slice(0, elem_count)
    store_split(force_ref, every, force * stiffness_ref[...])
    total = jnp.zeros((6 * high_count, LANES), f32)
    for corner in range(corners):
        row = connect_ref[corner : corner + 1, :]
        placed = scatter_rows(*split_rows(force_ref, corner, 3 * corners, every), row // LANES, high_count)
        total = total + nt_dot(placed, low_table(row))
    out_ref[...] = total[: 3 * high_count] + total[3 * high_count :]


def table_kernel(
    vol_ref, odd_ref, shape_ref, owner_ref, segment_ref, face_area_ref, face_ref, table_ref, rows_ref, area_ref, nodes_ref, both_ref, *, place_owner, groups
):
    order = shape_ref.shape[1]
    per_row = both_ref.shape[1] // order
    segment = segment_ref[...]
    slot = segment % per_row
    rows_ref[0:1, :] = slot
    rows_ref[1:2, :] = segment
    for corner in range(face_ref.shape[0]):
        table_ref[corner * LANES : (corner + 1) * LANES, :] = low_table(face_ref[corner : corner + 1, :])
    for part, local in enumerate(place_owner(owner_ref[...], vol_ref[0], odd_ref[0])):
        group = jnp.where(local < 0, -1, local * groups + segment // per_row)
        first = 2 + 4 * part
        rows_ref[first : first + 1, :] = group
        rows_ref[first + 1 : first + 2, :] = jnp.where(local < 0, -1, group % per_row)
        rows_ref[first + 2 : first + 3, :] = jnp.where(local < 0, -1, (group // per_row) * per_row + slot)
        rows_ref[first + 3 : first + 4, :] = jnp.where(local < 0, -1, local * PACK_ROWS + segment)
    area_ref[...] = -face_area_ref[...]
    nodes_ref[...] = face_ref[...] // LANES
    sixteen = jnp.concatenate([shape_ref[...], jnp.zeros((16 - shape_ref.shape[0], order), f32)], axis=0)
    zero = jnp.zeros_like(sixteen)
    diagonal = [
        jnp.concatenate([sixteen if r == c else zero for c in range(per_row)], axis=1) for r in range(per_row)
    ]
    both_ref[...] = jnp.concatenate(split(jnp.concatenate(diagonal, axis=0)), axis=0)


def contact_kernel(*refs, payloads, past, last, part, owners, chunk, tile):
    refs = list(refs)

    def take(count):
        taken = refs[:count]
        del refs[:count]
        return taken

    payload_refs = take(payloads)
    disp_ref, rows_ref, both_ref = take(3)
    (past_ref,) = take(1) if past else (None,)
    if last:
        area_ref, nodes_ref, table_ref, inner_ref, parity_ref = take(5)
        out_ref, near_ref, far_ref = take(3)
    else:
        (out_ref,) = take(1)
    blocks_ref, offsets_ref, map_ref, nodal_ref = refs
    order, faces = disp_ref.shape
    width = blocks_ref.shape[1]
    block_rows = blocks_ref.shape[0] // owners
    piece = block_rows + PACK_ROWS
    per_row = width // order
    chunks = blocks_ref.shape[0] // order // chunk
    quads = chunk // per_row
    rows = chunk * order
    size = 16 * per_row

    def at(number, count):
        return pl.ds(number * count if isinstance(number, int) else pl.multiple_of(number * count, count), count)

    place = 0
    lines = []
    for ref in payload_refs:
        for begin in range(0, ref.shape[0], piece):
            blocks_ref[place * block_rows : (place + 1) * block_rows, :] = ref[begin : begin + block_rows, :]
            lines.append(ref[begin + block_rows : begin + piece, :order].astype(f32))
            place += 1
    offsets_ref[...] = jnp.transpose(jnp.concatenate(lines, axis=0)).astype(bf16)

    def build(number, _):
        product = nt_dot(both_ref[...], blocks_ref[at(number, rows), :])
        product = product[:size] + product[size:]
        for quad in range(quads):
            both = jnp.concatenate(split(product[:, quad * width : (quad + 1) * width]), axis=0)
            map_ref[number, quad * 2 * size : (quad + 1) * 2 * size, :] = both
        return 0

    def find_gap(index):
        cols = at(index, tile)
        slot = rows_ref[0:1, cols]
        group, inner, outer, target = [rows_ref[2 + 4 * part + k : 3 + 4 * part + k, cols] for k in range(4)]
        shape = (owners * PACK_ROWS, tile)
        picks = jnp.broadcast_to(target, shape) == lax.broadcasted_iota(i32, shape, 0)
        offset = jnp.dot(offsets_ref[...], picks.astype(f32).astype(bf16), preferred_element_type=f32)
        group_wide = jnp.broadcast_to(group, (order, tile))
        spread = jnp.concatenate([masked(disp_ref[:, cols], slot, place) for place in range(per_row)], axis=0)

        def add_gap(number, found):
            product = jnp.dot(blocks_ref[at(number, rows), :], spread, preferred_element_type=f32)
            for place in range(chunk):
                value = product[place * order : (place + 1) * order]
                found = jnp.where(group_wide == number * chunk + place, value, found)
            return found

        zero_gap = jnp.zeros((order, tile), f32)
        product = add_gap(0, zero_gap) if chunks == 1 else lax.fori_loop(0, chunks, add_gap, zero_gap)
        return index, offset - product, inner, outer

    def find_nodal(index, pressure, inner, outer):
        cols = at(index, tile)
        traction = jnp.maximum(pressure, 0.0) + jnp.log(1.0 + jnp.exp(-jnp.abs(pressure)))
        traction = traction.astype(bf16)
        pressed = jnp.concatenate([masked(traction, inner, place) for place in range(per_row)], axis=0)
        outer_wide = jnp.broadcast_to(outer, (16, tile))

        def add_nodal(number, found):
            product = jnp.dot(map_ref[number], pressed, preferred_element_type=f32)
            for quad in range(quads):
                for place in range(per_row):
                    row = quad * 2 * size + place * 16
                    value = product[row : row + 16] + product[row + size : row + size + 16]
                    key = (number * quads + quad) * per_row + place
                    found = jnp.where(outer_wide == key, value, found)
            return found

        nodal = past_ref[:, cols] if past else jnp.zeros((16, tile), f32)
        nodal = add_nodal(0, nodal) if chunks == 1 else lax.fori_loop(0, chunks, add_nodal, nodal)
        if not last:
            out_ref[:, cols] = nodal
        else:
            store_split(nodal_ref, cols, nodal * area_ref[:, cols])

    def scatter(index, total):
        if not last:
            return total
        cols = at(index, tile)
        high_count = inner_ref.shape[0] // 3
        placed, tables = [], []
        for corner in range(nodes_ref.shape[0]):
            halves = split_rows(nodal_ref, corner, 16, cols)
            placed.append(scatter_rows(*halves, nodes_ref[corner : corner + 1, cols], high_count))
            tables.append(table_ref[corner * LANES : (corner + 1) * LANES, cols])
        return total + nt_dot(jnp.concatenate(placed, axis=1), jnp.concatenate(tables, axis=1))

    total = jnp.zeros((2 * inner_ref.shape[0], LANES), f32) if last else 0
    count = faces // tile
    if chunks == 1:
        found = {}
        for turn in range(count + 2):
            if turn < count:
                found[turn] = find_gap(turn)
            if turn == 0:
                build(0, 0)
            if 0 <= turn - 1 < count:
                find_nodal(*found.pop(turn - 1))
            if 0 <= turn - 2:
                total = scatter(turn - 2, total)
    else:
        lax.fori_loop(0, chunks, build, 0)

        def step(index, total):
            find_nodal(*find_gap(index))
            return scatter(index, total)

        total = lax.fori_loop(0, count, step, total)
    if last:
        inner_rows = inner_ref.shape[0]
        unsummed = total[:inner_rows] + total[inner_rows:] + inner_ref[...]
        high_count = inner_rows // 3
        edge = near_ref.shape[1] // LANES
        odd = parity_ref[0] == 1
        for c in range(3):
            for high in range(high_count):
                line = unsummed[c * high_count + high : c * high_count + high + 1]
                out_ref[c : c + 1, high * LANES : (high + 1) * LANES] = line
            for high in range(edge):
                low = unsummed[c * high_count + high : c * high_count + high + 1]
                top = (c + 1) * high_count - edge + high
                up = unsummed[top : top + 1]
                lanes = slice(high * LANES, (high + 1) * LANES)
                near_ref[c : c + 1, lanes] = jnp.where(odd, low, up)
                far_ref[c : c + 1, lanes] = jnp.where(odd, up, low)


def vmem():
    return pl.BlockSpec(memory_space=pltpu.VMEM)


def smem():
    return pl.BlockSpec(memory_space=pltpu.SMEM)


def call(kernel, out_shape, specs, scratch=(), flops=0, limit=LIMIT):
    single = not isinstance(out_shape, (list, tuple))
    return pl.pallas_call(
        kernel,
        out_shape=out_shape,
        in_specs=specs,
        out_specs=vmem() if single else [vmem()] * len(out_shape),
        scratch_shapes=list(scratch),
        compiler_params=pltpu.CompilerParams(vmem_limit_bytes=limit),
        cost_estimate=pl.CostEstimate(flops=flops, bytes_accessed=1_000_000, transcendentals=0),
    )


STEPS = ((2, 6, 4, 1, 1, 1), (4, 2, 3, 1, 4, 4))


def arrivals(masks):
    one, two, three, early, late_two, late_three = masks
    return [0, one, early, early ^ one, two, three], [late_two ^ two, late_three ^ three]


def place_exchanged(owner, vol, odd_slab):
    apart = owner ^ vol
    places = []
    for even, odd in zip(*[arrivals(masks) for masks in STEPS]):
        place = jnp.full_like(apart, -1)
        for index, (even_mask, odd_mask) in enumerate(zip(even, odd)):
            place = jnp.where(apart == jnp.where(odd_slab == 1, odd_mask, even_mask), index, place)
        places.append(place)
    return places


def shards(
    face_disp,
    contact_owner,
    segment,
    face_area,
    face_nodes,
    mortar_blocks,
    gap_offset,
    shape_table,
    node_disp,
    stiffness,
    connect,
    elem_matrix,
):
    vol_count, slab_count = lax.axis_size("vol"), lax.axis_size("slab")
    segments, order, _ = mortar_blocks.shape
    faces = face_disp.shape[1]
    face_corners = face_nodes.shape[0]
    node_count = node_disp.shape[1]
    corners, elem_count = connect.shape
    high_count = node_count // LANES
    per_row = 256 // order
    groups = segments // per_row
    block_rows = groups * order
    width = per_row * order
    vol = lax.axis_index("vol").astype(i32).reshape(1)
    slab = lax.axis_index("slab")
    parity = (slab & 1).astype(i32).reshape(1)

    def payload_shape(owners):
        return jax.ShapeDtypeStruct((owners * (block_rows + PACK_ROWS), width), bf16)

    lead = call(lead_kernel, jax.ShapeDtypeStruct((8, LANES), f32), [], flops=20_000_000_000)()
    payload = call(pack_kernel, payload_shape(1), [vmem()] * 3, flops=20_000_000_000)(mortar_blocks, gap_offset, lead)

    exchanged = vol_count == 8
    if exchanged:
        place_owner, counts = place_exchanged, [6, 2]
    else:
        place_owner, counts = (lambda owner, *_: [owner]), [vol_count]

    tables, rows, area, nodes, both = call(
        functools.partial(table_kernel, place_owner=place_owner, groups=groups),
        [
            jax.ShapeDtypeStruct((face_corners * LANES, faces), bf16),
            jax.ShapeDtypeStruct((2 + 4 * len(counts), faces), i32),
            jax.ShapeDtypeStruct((1, faces), f32),
            jax.ShapeDtypeStruct((face_corners, faces), i32),
            jax.ShapeDtypeStruct((32 * per_row, width), bf16),
        ],
        [smem()] * 2 + [vmem()] * 5,
        flops=2_000_000_000,
    )(vol, parity, shape_table, contact_owner.reshape(1, faces), segment[None, :], face_area[None, :], face_nodes)

    internal = call(
        element_kernel,
        jax.ShapeDtypeStruct((3 * high_count, LANES), f32),
        [vmem()] * 4,
        [pltpu.VMEM((elem_count // LANES, 3 * corners, LANES), f32), pltpu.VMEM((6 * corners, elem_count), f32)],
        flops=2_000_000_000,
    )(node_disp, connect, stiffness[None, :], elem_matrix)

    if exchanged:
        def swap(values, masks):
            pairs = [
                (v * slab_count + s, (v ^ masks[s % 2]) * slab_count + s)
                for v in range(vol_count)
                for s in range(slab_count)
            ]
            return lax.ppermute(values, ("vol", "slab"), pairs)

        def join(*pieces):
            owners = sum(piece.shape[0] for piece in pieces if piece.shape[1] == width) // (block_rows + PACK_ROWS)
            return call(join_kernel, payload_shape(owners), [vmem()] * len(pieces))(*pieces)

        masks = list(zip(*STEPS))
        one, two, three = [swap(payload, masks[k]) for k in range(3)]
        early = swap(join(payload, one), masks[3])
        late = [swap(join(two, internal), masks[4]), swap(three, masks[5])]
        parts = [[payload, one, early, two, three], late]
    else:
        parts = [[lax.all_gather(payload, "vol", tiled=True)]]

    nodal = None
    for part, pieces in enumerate(parts):
        past, last = part > 0, part == len(parts) - 1
        owners = counts[part]
        chunk = min(CHUNK, owners * groups)
        tile = min(256 if last else 512, faces)
        operands = pieces + [face_disp, rows, both]
        specs = [vmem()] * len(operands)
        outs = jax.ShapeDtypeStruct((16, faces), f32)
        if past:
            operands.append(nodal)
            specs.append(vmem())
        if last:
            operands += [area, nodes, tables, internal, parity]
            specs += [vmem()] * 4 + [smem()]
            outs = [
                jax.ShapeDtypeStruct((3, node_count), f32),
                jax.ShapeDtypeStruct((3, SH), f32),
                jax.ShapeDtypeStruct((3, SH), f32),
            ]
        nodal = call(
            functools.partial(
                contact_kernel,
                payloads=len(pieces),
                past=past,
                last=last,
                part=part,
                owners=owners,
                chunk=chunk,
                tile=tile,
            ),
            outs,
            specs,
            [
                pltpu.VMEM((owners * block_rows, width), bf16),
                pltpu.VMEM((order, owners * PACK_ROWS), bf16),
                pltpu.VMEM((owners * groups // chunk, 32 * chunk, width), bf16),
                pltpu.VMEM((32, faces), f32),
            ],
            flops=1_000_000_000,
        )(*operands)
    unsummed, near_out, far_out = nodal
    near_pairs = [(i, i + 1) for i in range(0, slab_count - 1, 2)]
    far_pairs = [(i, i + 1) for i in range(1, slab_count - 1, 2)]
    if slab_count % 2 == 0:
        far_pairs.append((0, slab_count - 1))
    far_in = lax.ppermute(far_out, "slab", far_pairs + [(b, a) for a, b in far_pairs])
    near_in = lax.ppermute(near_out, "slab", near_pairs + [(b, a) for a, b in near_pairs])
    odd = parity[0] == 1
    inside = (slab > 0) & (slab < slab_count - 1) if slab_count % 2 == 0 else True
    far_in = jnp.where(inside, far_in, 0.0)
    lower = unsummed[:, :SH] + jnp.where(odd, near_in, far_in)
    upper = unsummed[:, node_count - SH :] + jnp.where(odd, far_in, near_in)
    return jnp.concatenate([lower, unsummed[:, SH : node_count - SH], upper], axis=1)


def solution(mesh):
    in_specs = (
        P(None, ("vol", "slab")),
        P(("vol", "slab"), None),
        P(("vol", "slab")),
        P(("vol", "slab")),
        P(None, ("vol", "slab")),
        P(("vol", "slab"), None, None),
        P(("vol", "slab"), None),
        P(),
        P(None, ("vol", "slab")),
        P(("vol", "slab")),
        P(None, ("vol", "slab")),
        P(),
    )
    out_specs = P(None, ("vol", "slab"))
    return jax.shard_map(shards, mesh=mesh, in_specs=in_specs, out_specs=out_specs, check_vma=False)
```

```python
import functools

import jax
import jax.numpy as jnp
from jax import lax
from jax.experimental import pallas as pl
from jax.experimental.pallas import tpu as pltpu
from jax.sharding import PartitionSpec as P

SH = 256
LANES = 128
PACK_ROWS = 8
CHUNK = 16
LIMIT = 16 * 1024 * 1024

f32, bf16, i32 = jnp.float32, jnp.bfloat16, jnp.int32


def split(values):
    high = values.astype(bf16)
    return high, (values - high.astype(f32)).astype(bf16)


def nt_dot(left, right):
    return lax.dot_general(left, right, (((1,), (1,)), ((), ())), preferred_element_type=f32)


def low_table(node_row):
    shape = (LANES, node_row.shape[1])
    low = jnp.broadcast_to((node_row % LANES).astype(f32).astype(bf16), shape)
    lines = lax.broadcasted_iota(i32, shape, 0).astype(f32).astype(bf16)
    return jnp.where(low == lines, jnp.ones((), bf16), jnp.zeros((), bf16))


def low_columns(node_row):
    pieces = []
    for start in range(0, node_row.shape[1], LANES):
        low = (node_row[:, start : start + LANES] % LANES).astype(f32)
        lines = jnp.transpose(jnp.broadcast_to(low, (LANES, LANES)))
        hit = lines == lax.broadcasted_iota(i32, (LANES, LANES), 1).astype(f32)
        pieces.append(hit.astype(f32).astype(bf16))
    return jnp.concatenate(pieces, axis=0)


def scatter_rows(highs, lows, high_row, high_count):
    shape = (high_count, high_row.shape[1])
    mask = jnp.broadcast_to(high_row, shape) == lax.broadcasted_iota(i32, shape, 0)
    rows = [jnp.where(mask, jnp.broadcast_to(v, shape), 0.0) for v in highs + lows]
    return jnp.concatenate(rows, axis=0).astype(bf16)


def store_split(ref, cols, values):
    high, low = split(values)
    size = values.shape[0]
    ref[:size, cols] = high.astype(f32)
    ref[size : 2 * size, cols] = low.astype(f32)


def split_rows(ref, corner, size, cols):
    rows = [3 * corner + c for c in range(3)]
    return [ref[r : r + 1, cols] for r in rows], [ref[size + r : size + r + 1, cols] for r in rows]


def masked(values, row, number):
    return values * (row == number).astype(f32).astype(bf16)


def lead_kernel(out_ref):
    out_ref[...] = jnp.zeros(out_ref.shape, f32)


def pack_kernel(mortar_ref, offset_ref, _, out_ref):
    segments, order, _ = mortar_ref.shape
    per_row = out_ref.shape[1] // order
    for first in range(0, segments, per_row):
        row = first // per_row * order
        blocks = [mortar_ref[first + place] for place in range(per_row)]
        out_ref[row : row + order, :] = jnp.concatenate(blocks, axis=1)
    rows = segments // per_row * order
    out_ref[rows:, :] = jnp.zeros((PACK_ROWS, out_ref.shape[1]), bf16)
    out_ref[rows : rows + segments, :order] = offset_ref[...]


def join_kernel(*refs):
    out_ref = refs[-1]
    place = 0
    for ref in refs[:-1]:
        if len(ref.shape) == 2 and ref.shape[1] == out_ref.shape[1]:
            out_ref[place : place + ref.shape[0], :] = ref[...]
            place += ref.shape[0]


def element_kernel(disp_ref, connect_ref, stiffness_ref, matrix_ref, out_ref, elem_ref, force_ref):
    node_count = disp_ref.shape[1]
    corners, elem_count = connect_ref.shape
    high_count = node_count // LANES
    for start in range(0, elem_count, LANES):
        index = connect_ref[:, start : start + LANES]
        high, low = index // LANES, index % LANES
        for comp in range(3):
            picked = jnp.zeros(index.shape, f32)
            for part in range(high_count):
                line = disp_ref[comp : comp + 1, part * LANES : (part + 1) * LANES]
                table = jnp.broadcast_to(line, (corners, LANES))
                found = jnp.take_along_axis(table, low, axis=1, mode="promise_in_bounds")
                picked = jnp.where(high == part, found, picked)
            elem_ref[start // LANES, pl.ds(comp, corners, stride=3), :] = picked
    m_high, m_low = split(matrix_ref[...])
    d_high, d_low = split(jnp.concatenate([elem_ref[k] for k in range(elem_count // LANES)], axis=1))
    force = (
        jnp.dot(m_high, d_high, preferred_element_type=f32)
        + jnp.dot(m_high, d_low, preferred_element_type=f32)
        + jnp.dot(m_low, d_high, preferred_element_type=f32)
    )
    every = slice(0, elem_count)
    store_split(force_ref, every, force * stiffness_ref[...])
    total = jnp.zeros((6 * high_count, LANES), f32)
    for corner in range(corners):
        row = connect_ref[corner : corner + 1, :]
        placed = scatter_rows(*split_rows(force_ref, corner, 3 * corners, every), row // LANES, high_count)
        total = total + nt_dot(placed, low_table(row))
    out_ref[...] = total[: 3 * high_count] + total[3 * high_count :]


def table_kernel(
    vol_ref, odd_ref, shape_ref, owner_ref, segment_ref, face_area_ref, face_ref, disp_ref, table_ref, rows_ref, area_ref, nodes_ref, both_ref, spread_ref, *, place_owner, groups
):
    order = shape_ref.shape[1]
    per_row = both_ref.shape[1] // order
    segment = segment_ref[...]
    slot = segment % per_row
    rows_ref[0:1, :] = slot
    rows_ref[1:2, :] = segment
    for corner in range(face_ref.shape[0]):
        faces = face_ref.shape[1]
        table_ref[corner * faces : (corner + 1) * faces, :] = low_columns(face_ref[corner : corner + 1, :])
    for part, local in enumerate(place_owner(owner_ref[...], vol_ref[0], odd_ref[0])):
        group = jnp.where(local < 0, -1, local * groups + segment // per_row)
        first = 2 + 4 * part
        rows_ref[first : first + 1, :] = group
        rows_ref[first + 1 : first + 2, :] = jnp.where(local < 0, -1, group % per_row)
        rows_ref[first + 2 : first + 3, :] = jnp.where(local < 0, -1, (group // per_row) * per_row + slot)
        rows_ref[first + 3 : first + 4, :] = jnp.where(local < 0, -1, local * PACK_ROWS + segment)
    for place in range(per_row):
        spread_ref[place * order : (place + 1) * order, :] = masked(disp_ref[...], slot, place)
    area_ref[...] = -face_area_ref[...]
    nodes_ref[...] = face_ref[...] // LANES
    sixteen = jnp.concatenate([shape_ref[...], jnp.zeros((16 - shape_ref.shape[0], order), f32)], axis=0)
    zero = jnp.zeros_like(sixteen)
    diagonal = [
        jnp.concatenate([sixteen if r == c else zero for c in range(per_row)], axis=1) for r in range(per_row)
    ]
    both_ref[...] = jnp.concatenate(split(jnp.concatenate(diagonal, axis=0)), axis=0)


def contact_kernel(*refs, payloads, past, last, part, owners, chunk, tile):
    refs = list(refs)

    def take(count):
        taken = refs[:count]
        del refs[:count]
        return taken

    payload_refs = take(payloads)
    disp_ref, rows_ref, both_ref = take(3)
    (past_ref,) = take(1) if past else (None,)
    if last:
        area_ref, nodes_ref, table_ref, inner_ref, parity_ref = take(5)
        out_ref, near_ref, far_ref = take(3)
    else:
        (out_ref,) = take(1)
    blocks_ref, offsets_ref, map_ref, nodal_ref = refs
    width, faces = disp_ref.shape
    order = offsets_ref.shape[0]
    block_rows = blocks_ref.shape[0] // owners
    piece = block_rows + PACK_ROWS
    per_row = width // order
    chunks = blocks_ref.shape[0] // order // chunk
    quads = chunk // per_row
    rows = chunk * order
    size = 16 * per_row

    def at(number, count):
        return pl.ds(number * count if isinstance(number, int) else pl.multiple_of(number * count, count), count)

    place = 0
    lines = []
    for ref in payload_refs:
        for begin in range(0, ref.shape[0], piece):
            blocks_ref[place * block_rows : (place + 1) * block_rows, :] = ref[begin : begin + block_rows, :]
            lines.append(ref[begin + block_rows : begin + piece, :order].astype(f32))
            place += 1
    offsets_ref[...] = jnp.transpose(jnp.concatenate(lines, axis=0)).astype(bf16)

    def build(number, _):
        product = nt_dot(both_ref[...], blocks_ref[at(number, rows), :])
        product = product[:size] + product[size:]
        for quad in range(quads):
            both = jnp.concatenate(split(product[:, quad * width : (quad + 1) * width]), axis=0)
            map_ref[number, quad * 2 * size : (quad + 1) * 2 * size, :] = both
        return 0

    def find_gap(index):
        cols = at(index, tile)
        group, inner, outer, target = [rows_ref[2 + 4 * part + k : 3 + 4 * part + k, cols] for k in range(4)]
        shape = (owners * PACK_ROWS, tile)
        picks = jnp.broadcast_to(target, shape) == lax.broadcasted_iota(i32, shape, 0)
        offset = jnp.dot(offsets_ref[...], picks.astype(f32).astype(bf16), preferred_element_type=f32)
        group_wide = jnp.broadcast_to(group, (order, tile))
        spread = disp_ref[:, cols]

        def add_gap(number, found):
            product = jnp.dot(blocks_ref[at(number, rows), :], spread, preferred_element_type=f32)
            for place in range(chunk):
                value = product[place * order : (place + 1) * order]
                found = jnp.where(group_wide == number * chunk + place, value, found)
            return found

        zero_gap = jnp.zeros((order, tile), f32)
        product = add_gap(0, zero_gap) if chunks == 1 else lax.fori_loop(0, chunks, add_gap, zero_gap)
        return index, offset - product, inner, outer

    def find_nodal(index, pressure, inner, outer):
        cols = at(index, tile)
        traction = jnp.maximum(pressure, 0.0) + jnp.log(1.0 + jnp.exp(-jnp.abs(pressure)))
        traction = traction.astype(bf16)
        pressed = jnp.concatenate([masked(traction, inner, place) for place in range(per_row)], axis=0)
        outer_wide = jnp.broadcast_to(outer, (16, tile))

        def add_nodal(number, found):
            product = jnp.dot(map_ref[number], pressed, preferred_element_type=f32)
            for quad in range(quads):
                for place in range(per_row):
                    row = quad * 2 * size + place * 16
                    value = product[row : row + 16] + product[row + size : row + size + 16]
                    key = (number * quads + quad) * per_row + place
                    found = jnp.where(outer_wide == key, value, found)
            return found

        nodal = past_ref[:, cols] if past else jnp.zeros((16, tile), f32)
        nodal = add_nodal(0, nodal) if chunks == 1 else lax.fori_loop(0, chunks, add_nodal, nodal)
        if not last:
            out_ref[:, cols] = nodal
        else:
            store_split(nodal_ref, cols, nodal * area_ref[:, cols])

    def scatter(index, total):
        if not last:
            return total
        cols = at(index, tile)
        high_count = inner_ref.shape[0] // 3
        placed, tables = [], []
        for corner in range(nodes_ref.shape[0]):
            halves = split_rows(nodal_ref, corner, 16, cols)
            placed.append(scatter_rows(*halves, nodes_ref[corner : corner + 1, cols], high_count))
            begin = corner * faces + index * tile
            begin = begin if isinstance(index, int) else pl.multiple_of(begin, tile)
            tables.append(table_ref[pl.ds(begin, tile), :])
        return total + jnp.dot(
            jnp.concatenate(placed, axis=1), jnp.concatenate(tables, axis=0), preferred_element_type=f32
        )

    total = jnp.zeros((2 * inner_ref.shape[0], LANES), f32) if last else 0
    count = faces // tile
    if chunks == 1:
        found = {}
        for turn in range(count + 2):
            if turn < count:
                found[turn] = find_gap(turn)
            if turn == 0:
                build(0, 0)
            if 0 <= turn - 1 < count:
                find_nodal(*found.pop(turn - 1))
            if 0 <= turn - 2:
                total = scatter(turn - 2, total)
    else:
        lax.fori_loop(0, chunks, build, 0)

        def step(index, total):
            find_nodal(*find_gap(index))
            return scatter(index, total)

        total = lax.fori_loop(0, count, step, total)
    if last:
        inner_rows = inner_ref.shape[0]
        unsummed = total[:inner_rows] + total[inner_rows:] + inner_ref[...]
        high_count = inner_rows // 3
        edge = near_ref.shape[1] // LANES
        odd = parity_ref[0] == 1
        for c in range(3):
            for high in range(high_count):
                line = unsummed[c * high_count + high : c * high_count + high + 1]
                out_ref[c : c + 1, high * LANES : (high + 1) * LANES] = line
            for high in range(edge):
                low = unsummed[c * high_count + high : c * high_count + high + 1]
                top = (c + 1) * high_count - edge + high
                up = unsummed[top : top + 1]
                lanes = slice(high * LANES, (high + 1) * LANES)
                near_ref[c : c + 1, lanes] = jnp.where(odd, low, up)
                far_ref[c : c + 1, lanes] = jnp.where(odd, up, low)


def vmem():
    return pl.BlockSpec(memory_space=pltpu.VMEM)


def smem():
    return pl.BlockSpec(memory_space=pltpu.SMEM)


def call(kernel, out_shape, specs, scratch=(), flops=0, limit=LIMIT):
    single = not isinstance(out_shape, (list, tuple))
    return pl.pallas_call(
        kernel,
        out_shape=out_shape,
        in_specs=specs,
        out_specs=vmem() if single else [vmem()] * len(out_shape),
        scratch_shapes=list(scratch),
        compiler_params=pltpu.CompilerParams(vmem_limit_bytes=limit),
        cost_estimate=pl.CostEstimate(flops=flops, bytes_accessed=1_000_000, transcendentals=0),
    )


STEPS = ((2, 6, 4, 1, 1, 1), (4, 2, 3, 1, 4, 4))


def arrivals(masks):
    one, two, three, early, late_two, late_three = masks
    return [0, one, early, early ^ one, two, three], [late_two ^ two, late_three ^ three]


def place_exchanged(owner, vol, odd_slab):
    apart = owner ^ vol
    places = []
    for even, odd in zip(*[arrivals(masks) for masks in STEPS]):
        place = jnp.full_like(apart, -1)
        for index, (even_mask, odd_mask) in enumerate(zip(even, odd)):
            place = jnp.where(apart == jnp.where(odd_slab == 1, odd_mask, even_mask), index, place)
        places.append(place)
    return places


def shards(
    face_disp,
    contact_owner,
    segment,
    face_area,
    face_nodes,
    mortar_blocks,
    gap_offset,
    shape_table,
    node_disp,
    stiffness,
    connect,
    elem_matrix,
):
    vol_count, slab_count = lax.axis_size("vol"), lax.axis_size("slab")
    segments, order, _ = mortar_blocks.shape
    faces = face_disp.shape[1]
    face_corners = face_nodes.shape[0]
    node_count = node_disp.shape[1]
    corners, elem_count = connect.shape
    high_count = node_count // LANES
    per_row = 256 // order
    groups = segments // per_row
    block_rows = groups * order
    width = per_row * order
    vol = lax.axis_index("vol").astype(i32).reshape(1)
    slab = lax.axis_index("slab")
    parity = (slab & 1).astype(i32).reshape(1)

    def payload_shape(owners):
        return jax.ShapeDtypeStruct((owners * (block_rows + PACK_ROWS), width), bf16)

    lead = call(lead_kernel, jax.ShapeDtypeStruct((8, LANES), f32), [], flops=20_000_000_000)()
    payload = call(pack_kernel, payload_shape(1), [vmem()] * 3, flops=20_000_000_000)(mortar_blocks, gap_offset, lead)

    exchanged = vol_count == 8
    if exchanged:
        place_owner, counts = place_exchanged, [6, 2]
    else:
        place_owner, counts = (lambda owner, *_: [owner]), [vol_count]

    tables, rows, area, nodes, both, spread = call(
        functools.partial(table_kernel, place_owner=place_owner, groups=groups),
        [
            jax.ShapeDtypeStruct((face_corners * faces, LANES), bf16),
            jax.ShapeDtypeStruct((2 + 4 * len(counts), faces), i32),
            jax.ShapeDtypeStruct((1, faces), f32),
            jax.ShapeDtypeStruct((face_corners, faces), i32),
            jax.ShapeDtypeStruct((32 * per_row, width), bf16),
            jax.ShapeDtypeStruct((width, faces), bf16),
        ],
        [smem()] * 2 + [vmem()] * 6,
        flops=2_000_000_000,
    )(vol, parity, shape_table, contact_owner.reshape(1, faces), segment[None, :], face_area[None, :], face_nodes, face_disp)

    internal = call(
        element_kernel,
        jax.ShapeDtypeStruct((3 * high_count, LANES), f32),
        [vmem()] * 4,
        [pltpu.VMEM((elem_count // LANES, 3 * corners, LANES), f32), pltpu.VMEM((6 * corners, elem_count), f32)],
        flops=2_000_000_000,
    )(node_disp, connect, stiffness[None, :], elem_matrix)

    if exchanged:
        def swap(values, masks):
            pairs = [
                (v * slab_count + s, (v ^ masks[s % 2]) * slab_count + s)
                for v in range(vol_count)
                for s in range(slab_count)
            ]
            return lax.ppermute(values, ("vol", "slab"), pairs)

        def join(*pieces):
            owners = sum(piece.shape[0] for piece in pieces if piece.shape[1] == width) // (block_rows + PACK_ROWS)
            return call(join_kernel, payload_shape(owners), [vmem()] * len(pieces))(*pieces)

        masks = list(zip(*STEPS))
        one, two, three = [swap(payload, masks[k]) for k in range(3)]
        early = swap(join(payload, one), masks[3])
        late = [swap(join(two, internal), masks[4]), swap(three, masks[5])]
        parts = [[payload, one, early, two, three], late]
    else:
        parts = [[lax.all_gather(payload, "vol", tiled=True)]]

    nodal = None
    for part, pieces in enumerate(parts):
        past, last = part > 0, part == len(parts) - 1
        owners = counts[part]
        chunk = min(CHUNK, owners * groups)
        tile = min(512 if last else 1024, faces)
        operands = pieces + [spread, rows, both]
        specs = [vmem()] * len(operands)
        outs = jax.ShapeDtypeStruct((16, faces), f32)
        if past:
            operands.append(nodal)
            specs.append(vmem())
        if last:
            operands += [area, nodes, tables, internal, parity]
            specs += [vmem()] * 4 + [smem()]
            outs = [
                jax.ShapeDtypeStruct((3, node_count), f32),
                jax.ShapeDtypeStruct((3, SH), f32),
                jax.ShapeDtypeStruct((3, SH), f32),
            ]
        nodal = call(
            functools.partial(
                contact_kernel,
                payloads=len(pieces),
                past=past,
                last=last,
                part=part,
                owners=owners,
                chunk=chunk,
                tile=tile,
            ),
            outs,
            specs,
            [
                pltpu.VMEM((owners * block_rows, width), bf16),
                pltpu.VMEM((order, owners * PACK_ROWS), bf16),
                pltpu.VMEM((owners * groups // chunk, 32 * chunk, width), bf16),
                pltpu.VMEM((32, faces), f32),
            ],
            flops=1_000_000_000,
        )(*operands)
    unsummed, near_out, far_out = nodal
    near_pairs = [(i, i + 1) for i in range(0, slab_count - 1, 2)]
    far_pairs = [(i, i + 1) for i in range(1, slab_count - 1, 2)]
    if slab_count % 2 == 0:
        far_pairs.append((0, slab_count - 1))
    far_in = lax.ppermute(far_out, "slab", far_pairs + [(b, a) for a, b in far_pairs])
    near_in = lax.ppermute(near_out, "slab", near_pairs + [(b, a) for a, b in near_pairs])
    odd = parity[0] == 1
    inside = (slab > 0) & (slab < slab_count - 1) if slab_count % 2 == 0 else True
    far_in = jnp.where(inside, far_in, 0.0)
    lower = unsummed[:, :SH] + jnp.where(odd, near_in, far_in)
    upper = unsummed[:, node_count - SH :] + jnp.where(odd, far_in, near_in)
    return jnp.concatenate([lower, unsummed[:, SH : node_count - SH], upper], axis=1)


def solution(mesh):
    in_specs = (
        P(None, ("vol", "slab")),
        P(("vol", "slab"), None),
        P(("vol", "slab")),
        P(("vol", "slab")),
        P(None, ("vol", "slab")),
        P(("vol", "slab"), None, None),
        P(("vol", "slab"), None),
        P(),
        P(None, ("vol", "slab")),
        P(("vol", "slab")),
        P(None, ("vol", "slab")),
        P(),
    )
    out_specs = P(None, ("vol", "slab"))
    return jax.shard_map(shards, mesh=mesh, in_specs=in_specs, out_specs=out_specs, check_vma=False)
```

```python
import functools

import jax
import jax.numpy as jnp
from jax import lax
from jax.experimental import pallas as pl
from jax.experimental.pallas import tpu as pltpu
from jax.sharding import PartitionSpec as P

SH = 256
LANES = 128
PACK_ROWS = 8
CHUNK = 16
LIMIT = 16 * 1024 * 1024

f32, bf16, i32 = jnp.float32, jnp.bfloat16, jnp.int32


def split(values):
    high = values.astype(bf16)
    return high, (values - high.astype(f32)).astype(bf16)


def nt_dot(left, right):
    return lax.dot_general(left, right, (((1,), (1,)), ((), ())), preferred_element_type=f32)


def low_table(node_row):
    shape = (LANES, node_row.shape[1])
    low = jnp.broadcast_to((node_row % LANES).astype(f32).astype(bf16), shape)
    lines = lax.broadcasted_iota(i32, shape, 0).astype(f32).astype(bf16)
    return jnp.where(low == lines, jnp.ones((), bf16), jnp.zeros((), bf16))


def low_columns(node_row):
    table = low_table(node_row)
    pieces = [jnp.transpose(table[:, start : start + LANES]) for start in range(0, node_row.shape[1], LANES)]
    return jnp.concatenate(pieces, axis=0)


def scatter_rows(highs, lows, high_row, high_count):
    shape = (high_count, high_row.shape[1])
    mask = jnp.broadcast_to(high_row, shape) == lax.broadcasted_iota(i32, shape, 0)
    rows = [jnp.where(mask, jnp.broadcast_to(v, shape), 0.0) for v in highs + lows]
    return jnp.concatenate(rows, axis=0).astype(bf16)


def store_split(ref, cols, values):
    high, low = split(values)
    size = values.shape[0]
    ref[:size, cols] = high.astype(f32)
    ref[size : 2 * size, cols] = low.astype(f32)


def split_rows(ref, corner, size, cols):
    rows = [3 * corner + c for c in range(3)]
    return [ref[r : r + 1, cols] for r in rows], [ref[size + r : size + r + 1, cols] for r in rows]


def masked(values, row, number):
    return values * (row == number).astype(f32).astype(bf16)


def lead_kernel(out_ref):
    out_ref[...] = jnp.zeros(out_ref.shape, f32)


def pack_kernel(mortar_ref, offset_ref, _, out_ref):
    segments, order, _ = mortar_ref.shape
    per_row = out_ref.shape[1] // order
    for first in range(0, segments, per_row):
        row = first // per_row * order
        blocks = [mortar_ref[first + place] for place in range(per_row)]
        out_ref[row : row + order, :] = jnp.concatenate(blocks, axis=1)
    rows = segments // per_row * order
    out_ref[rows:, :] = jnp.zeros((PACK_ROWS, out_ref.shape[1]), bf16)
    out_ref[rows : rows + segments, :order] = offset_ref[...]


def join_kernel(*refs):
    out_ref = refs[-1]
    place = 0
    for ref in refs[:-1]:
        if len(ref.shape) == 2 and ref.shape[1] == out_ref.shape[1]:
            out_ref[place : place + ref.shape[0], :] = ref[...]
            place += ref.shape[0]


def element_kernel(disp_ref, connect_ref, stiffness_ref, matrix_ref, out_ref, elem_ref, force_ref):
    node_count = disp_ref.shape[1]
    corners, elem_count = connect_ref.shape
    high_count = node_count // LANES
    for start in range(0, elem_count, LANES):
        index = connect_ref[:, start : start + LANES]
        high, low = index // LANES, index % LANES
        for comp in range(3):
            picked = jnp.zeros(index.shape, f32)
            for part in range(high_count):
                line = disp_ref[comp : comp + 1, part * LANES : (part + 1) * LANES]
                table = jnp.broadcast_to(line, (corners, LANES))
                found = jnp.take_along_axis(table, low, axis=1, mode="promise_in_bounds")
                picked = jnp.where(high == part, found, picked)
            elem_ref[start // LANES, pl.ds(comp, corners, stride=3), :] = picked
    m_high, m_low = split(matrix_ref[...])
    d_high, d_low = split(jnp.concatenate([elem_ref[k] for k in range(elem_count // LANES)], axis=1))
    force = (
        jnp.dot(m_high, d_high, preferred_element_type=f32)
        + jnp.dot(m_high, d_low, preferred_element_type=f32)
        + jnp.dot(m_low, d_high, preferred_element_type=f32)
    )
    every = slice(0, elem_count)
    store_split(force_ref, every, force * stiffness_ref[...])
    total = jnp.zeros((6 * high_count, LANES), f32)
    for corner in range(corners):
        row = connect_ref[corner : corner + 1, :]
        placed = scatter_rows(*split_rows(force_ref, corner, 3 * corners, every), row // LANES, high_count)
        total = total + nt_dot(placed, low_table(row))
    out_ref[...] = total[: 3 * high_count] + total[3 * high_count :]


def table_kernel(
    vol_ref, odd_ref, shape_ref, owner_ref, segment_ref, face_area_ref, face_ref, disp_ref, table_ref, rows_ref, area_ref, nodes_ref, both_ref, spread_ref, *, place_owner, groups
):
    order = shape_ref.shape[1]
    per_row = both_ref.shape[1] // order
    segment = segment_ref[...]
    slot = segment % per_row
    rows_ref[0:1, :] = slot
    rows_ref[1:2, :] = segment
    for corner in range(face_ref.shape[0]):
        faces = face_ref.shape[1]
        table_ref[corner * faces : (corner + 1) * faces, :] = low_columns(face_ref[corner : corner + 1, :])
    for part, local in enumerate(place_owner(owner_ref[...], vol_ref[0], odd_ref[0])):
        group = jnp.where(local < 0, -1, local * groups + segment // per_row)
        first = 2 + 4 * part
        rows_ref[first : first + 1, :] = group
        rows_ref[first + 1 : first + 2, :] = jnp.where(local < 0, -1, group % per_row)
        rows_ref[first + 2 : first + 3, :] = jnp.where(local < 0, -1, (group // per_row) * per_row + slot)
        rows_ref[first + 3 : first + 4, :] = jnp.where(local < 0, -1, local * PACK_ROWS + segment)
    for place in range(per_row):
        spread_ref[place * order : (place + 1) * order, :] = masked(disp_ref[...], slot, place)
    area_ref[...] = -face_area_ref[...]
    nodes_ref[...] = face_ref[...] // LANES
    sixteen = jnp.concatenate([shape_ref[...], jnp.zeros((16 - shape_ref.shape[0], order), f32)], axis=0)
    zero = jnp.zeros_like(sixteen)
    diagonal = [
        jnp.concatenate([sixteen if r == c else zero for c in range(per_row)], axis=1) for r in range(per_row)
    ]
    both_ref[...] = jnp.concatenate(split(jnp.concatenate(diagonal, axis=0)), axis=0)


def contact_kernel(*refs, payloads, past, last, part, owners, chunk, tile):
    refs = list(refs)

    def take(count):
        taken = refs[:count]
        del refs[:count]
        return taken

    payload_refs = take(payloads)
    disp_ref, rows_ref, both_ref = take(3)
    (past_ref,) = take(1) if past else (None,)
    if last:
        area_ref, nodes_ref, table_ref, inner_ref, parity_ref = take(5)
        out_ref, near_ref, far_ref = take(3)
    else:
        (out_ref,) = take(1)
    blocks_ref, offsets_ref, map_ref, nodal_ref = refs
    width, faces = disp_ref.shape
    order = offsets_ref.shape[0]
    block_rows = blocks_ref.shape[0] // owners
    piece = block_rows + PACK_ROWS
    per_row = width // order
    chunks = blocks_ref.shape[0] // order // chunk
    quads = chunk // per_row
    rows = chunk * order
    size = 16 * per_row

    def at(number, count):
        return pl.ds(number * count if isinstance(number, int) else pl.multiple_of(number * count, count), count)

    place = 0
    lines = []
    for ref in payload_refs:
        for begin in range(0, ref.shape[0], piece):
            blocks_ref[place * block_rows : (place + 1) * block_rows, :] = ref[begin : begin + block_rows, :]
            lines.append(ref[begin + block_rows : begin + piece, :order].astype(f32))
            place += 1
    offsets_ref[...] = jnp.transpose(jnp.concatenate(lines, axis=0)).astype(bf16)

    def build(number, _):
        product = nt_dot(both_ref[...], blocks_ref[at(number, rows), :])
        product = product[:size] + product[size:]
        for quad in range(quads):
            both = jnp.concatenate(split(product[:, quad * width : (quad + 1) * width]), axis=0)
            map_ref[number, quad * 2 * size : (quad + 1) * 2 * size, :] = both
        return 0

    def find_gap(index):
        cols = at(index, tile)
        group, inner, outer, target = [rows_ref[2 + 4 * part + k : 3 + 4 * part + k, cols] for k in range(4)]
        shape = (owners * PACK_ROWS, tile)
        picks = jnp.broadcast_to(target, shape) == lax.broadcasted_iota(i32, shape, 0)
        offset = jnp.dot(offsets_ref[...], picks.astype(f32).astype(bf16), preferred_element_type=f32)
        group_wide = jnp.broadcast_to(group, (order, tile))
        spread = disp_ref[:, cols]

        def add_gap(number, found):
            product = jnp.dot(blocks_ref[at(number, rows), :], spread, preferred_element_type=f32)
            for place in range(chunk):
                value = product[place * order : (place + 1) * order]
                found = jnp.where(group_wide == number * chunk + place, value, found)
            return found

        zero_gap = jnp.zeros((order, tile), f32)
        product = add_gap(0, zero_gap) if chunks == 1 else lax.fori_loop(0, chunks, add_gap, zero_gap)
        return index, offset - product, inner, outer

    def find_nodal(index, pressure, inner, outer):
        cols = at(index, tile)
        traction = jnp.maximum(pressure, 0.0) + jnp.log(1.0 + jnp.exp(-jnp.abs(pressure)))
        traction = traction.astype(bf16)
        pressed = jnp.concatenate([masked(traction, inner, place) for place in range(per_row)], axis=0)
        outer_wide = jnp.broadcast_to(outer, (16, tile))

        def add_nodal(number, found):
            product = jnp.dot(map_ref[number], pressed, preferred_element_type=f32)
            for quad in range(quads):
                for place in range(per_row):
                    row = quad * 2 * size + place * 16
                    value = product[row : row + 16] + product[row + size : row + size + 16]
                    key = (number * quads + quad) * per_row + place
                    found = jnp.where(outer_wide == key, value, found)
            return found

        nodal = past_ref[:, cols] if past else jnp.zeros((16, tile), f32)
        nodal = add_nodal(0, nodal) if chunks == 1 else lax.fori_loop(0, chunks, add_nodal, nodal)
        if not last:
            out_ref[:, cols] = nodal
        else:
            store_split(nodal_ref, cols, nodal * area_ref[:, cols])

    def scatter(index, total):
        if not last:
            return total
        cols = at(index, tile)
        high_count = inner_ref.shape[0] // 3
        placed, tables = [], []
        for corner in range(nodes_ref.shape[0]):
            halves = split_rows(nodal_ref, corner, 16, cols)
            placed.append(scatter_rows(*halves, nodes_ref[corner : corner + 1, cols], high_count))
            begin = corner * faces + index * tile
            begin = begin if isinstance(index, int) else pl.multiple_of(begin, tile)
            tables.append(table_ref[pl.ds(begin, tile), :])
        return total + jnp.dot(
            jnp.concatenate(placed, axis=1), jnp.concatenate(tables, axis=0), preferred_element_type=f32
        )

    total = jnp.zeros((2 * inner_ref.shape[0], LANES), f32) if last else 0
    count = faces // tile
    if chunks == 1:
        found = {}
        for turn in range(count + 2):
            if turn < count:
                found[turn] = find_gap(turn)
            if turn == 0:
                build(0, 0)
            if 0 <= turn - 1 < count:
                find_nodal(*found.pop(turn - 1))
            if 0 <= turn - 2:
                total = scatter(turn - 2, total)
    else:
        lax.fori_loop(0, chunks, build, 0)

        def step(index, total):
            find_nodal(*find_gap(index))
            return scatter(index, total)

        total = lax.fori_loop(0, count, step, total)
    if last:
        inner_rows = inner_ref.shape[0]
        unsummed = total[:inner_rows] + total[inner_rows:] + inner_ref[...]
        high_count = inner_rows // 3
        edge = near_ref.shape[1] // LANES
        odd = parity_ref[0] == 1
        for c in range(3):
            for high in range(high_count):
                line = unsummed[c * high_count + high : c * high_count + high + 1]
                out_ref[c : c + 1, high * LANES : (high + 1) * LANES] = line
            for high in range(edge):
                low = unsummed[c * high_count + high : c * high_count + high + 1]
                top = (c + 1) * high_count - edge + high
                up = unsummed[top : top + 1]
                lanes = slice(high * LANES, (high + 1) * LANES)
                near_ref[c : c + 1, lanes] = jnp.where(odd, low, up)
                far_ref[c : c + 1, lanes] = jnp.where(odd, up, low)


def vmem():
    return pl.BlockSpec(memory_space=pltpu.VMEM)


def smem():
    return pl.BlockSpec(memory_space=pltpu.SMEM)


def call(kernel, out_shape, specs, scratch=(), flops=0, limit=LIMIT):
    single = not isinstance(out_shape, (list, tuple))
    return pl.pallas_call(
        kernel,
        out_shape=out_shape,
        in_specs=specs,
        out_specs=vmem() if single else [vmem()] * len(out_shape),
        scratch_shapes=list(scratch),
        compiler_params=pltpu.CompilerParams(vmem_limit_bytes=limit),
        cost_estimate=pl.CostEstimate(flops=flops, bytes_accessed=1_000_000, transcendentals=0),
    )


STEPS = ((2, 6, 4, 1, 1, 1), (4, 3, 2, 1, 4, 4))


def arrivals(masks):
    one, two, three, early, late_two, late_three = masks
    return [0, one, early, early ^ one, two, three], [late_two ^ two, late_three ^ three]


def place_exchanged(owner, vol, odd_slab):
    apart = owner ^ vol
    places = []
    for even, odd in zip(*[arrivals(masks) for masks in STEPS]):
        place = jnp.full_like(apart, -1)
        for index, (even_mask, odd_mask) in enumerate(zip(even, odd)):
            place = jnp.where(apart == jnp.where(odd_slab == 1, odd_mask, even_mask), index, place)
        places.append(place)
    return places


def shards(
    face_disp,
    contact_owner,
    segment,
    face_area,
    face_nodes,
    mortar_blocks,
    gap_offset,
    shape_table,
    node_disp,
    stiffness,
    connect,
    elem_matrix,
):
    vol_count, slab_count = lax.axis_size("vol"), lax.axis_size("slab")
    segments, order, _ = mortar_blocks.shape
    faces = face_disp.shape[1]
    face_corners = face_nodes.shape[0]
    node_count = node_disp.shape[1]
    corners, elem_count = connect.shape
    high_count = node_count // LANES
    per_row = 256 // order
    groups = segments // per_row
    block_rows = groups * order
    width = per_row * order
    vol = lax.axis_index("vol").astype(i32).reshape(1)
    slab = lax.axis_index("slab")
    parity = (slab & 1).astype(i32).reshape(1)

    def payload_shape(owners):
        return jax.ShapeDtypeStruct((owners * (block_rows + PACK_ROWS), width), bf16)

    lead = call(lead_kernel, jax.ShapeDtypeStruct((8, LANES), f32), [], flops=20_000_000_000)()
    payload = call(pack_kernel, payload_shape(1), [vmem()] * 3, flops=20_000_000_000)(mortar_blocks, gap_offset, lead)

    exchanged = vol_count == 8
    if exchanged:
        place_owner, counts = place_exchanged, [6, 2]
    else:
        place_owner, counts = (lambda owner, *_: [owner]), [vol_count]

    tables, rows, area, nodes, both, spread = call(
        functools.partial(table_kernel, place_owner=place_owner, groups=groups),
        [
            jax.ShapeDtypeStruct((face_corners * faces, LANES), bf16),
            jax.ShapeDtypeStruct((2 + 4 * len(counts), faces), i32),
            jax.ShapeDtypeStruct((1, faces), f32),
            jax.ShapeDtypeStruct((face_corners, faces), i32),
            jax.ShapeDtypeStruct((32 * per_row, width), bf16),
            jax.ShapeDtypeStruct((width, faces), bf16),
        ],
        [smem()] * 2 + [vmem()] * 6,
        flops=2_000_000_000,
    )(vol, parity, shape_table, contact_owner.reshape(1, faces), segment[None, :], face_area[None, :], face_nodes, face_disp)

    internal = call(
        element_kernel,
        jax.ShapeDtypeStruct((3 * high_count, LANES), f32),
        [vmem()] * 4,
        [pltpu.VMEM((elem_count // LANES, 3 * corners, LANES), f32), pltpu.VMEM((6 * corners, elem_count), f32)],
        flops=2_000_000_000,
    )(node_disp, connect, stiffness[None, :], elem_matrix)

    if exchanged:
        def swap(values, masks):
            pairs = [
                (v * slab_count + s, (v ^ masks[s % 2]) * slab_count + s)
                for v in range(vol_count)
                for s in range(slab_count)
            ]
            return lax.ppermute(values, ("vol", "slab"), pairs)

        def join(*pieces):
            owners = sum(piece.shape[0] for piece in pieces if piece.shape[1] == width) // (block_rows + PACK_ROWS)
            return call(join_kernel, payload_shape(owners), [vmem()] * len(pieces))(*pieces)

        masks = list(zip(*STEPS))
        one, two, three = [swap(payload, masks[k]) for k in range(3)]
        early = swap(join(payload, one), masks[3])
        late = [swap(lax.optimization_barrier((two, internal))[0], masks[4]), swap(three, masks[5])]
        parts = [[payload, one, early, two, three], late]
    else:
        parts = [[lax.all_gather(payload, "vol", tiled=True)]]

    nodal = None
    for part, pieces in enumerate(parts):
        past, last = part > 0, part == len(parts) - 1
        owners = counts[part]
        chunk = min(CHUNK, owners * groups)
        tile = min(512 if last else 1024, faces)
        operands = pieces + [spread, rows, both]
        specs = [vmem()] * len(operands)
        outs = jax.ShapeDtypeStruct((16, faces), f32)
        if past:
            operands.append(nodal)
            specs.append(vmem())
        if last:
            operands += [area, nodes, tables, internal, parity]
            specs += [vmem()] * 4 + [smem()]
            outs = [
                jax.ShapeDtypeStruct((3, node_count), f32),
                jax.ShapeDtypeStruct((3, SH), f32),
                jax.ShapeDtypeStruct((3, SH), f32),
            ]
        nodal = call(
            functools.partial(
                contact_kernel,
                payloads=len(pieces),
                past=past,
                last=last,
                part=part,
                owners=owners,
                chunk=chunk,
                tile=tile,
            ),
            outs,
            specs,
            [
                pltpu.VMEM((owners * block_rows, width), bf16),
                pltpu.VMEM((order, owners * PACK_ROWS), bf16),
                pltpu.VMEM((owners * groups // chunk, 32 * chunk, width), bf16),
                pltpu.VMEM((32, faces), f32),
            ],
            flops=1_000_000_000,
        )(*operands)
    unsummed, near_out, far_out = nodal
    near_pairs = [(i, i + 1) for i in range(0, slab_count - 1, 2)]
    far_pairs = [(i, i + 1) for i in range(1, slab_count - 1, 2)]
    if slab_count % 2 == 0:
        far_pairs.append((0, slab_count - 1))
    far_in = lax.ppermute(far_out, "slab", far_pairs + [(b, a) for a, b in far_pairs])
    near_in = lax.ppermute(near_out, "slab", near_pairs + [(b, a) for a, b in near_pairs])
    odd = parity[0] == 1
    inside = (slab > 0) & (slab < slab_count - 1) if slab_count % 2 == 0 else True
    far_in = jnp.where(inside, far_in, 0.0)
    lower = unsummed[:, :SH] + jnp.where(odd, near_in, far_in)
    upper = unsummed[:, node_count - SH :] + jnp.where(odd, far_in, near_in)
    return jnp.concatenate([lower, unsummed[:, SH : node_count - SH], upper], axis=1)


def solution(mesh):
    in_specs = (
        P(None, ("vol", "slab")),
        P(("vol", "slab"), None),
        P(("vol", "slab")),
        P(("vol", "slab")),
        P(None, ("vol", "slab")),
        P(("vol", "slab"), None, None),
        P(("vol", "slab"), None),
        P(),
        P(None, ("vol", "slab")),
        P(("vol", "slab")),
        P(None, ("vol", "slab")),
        P(),
    )
    out_specs = P(None, ("vol", "slab"))
    return jax.shard_map(shards, mesh=mesh, in_specs=in_specs, out_specs=out_specs, check_vma=False)
```
